128 devices in a mesh: dp: 16 (over z, x), expert: 8 (over y, core).
Axes of the slice: x: 4, y: 4, z: 4, core: 2. Of those that a mesh axis runs over, the one named last changes fastest.
Arguments:
- grads: bfloat16 [16, 4096, 6144], P('dp', None, 'expert'), parts along dimension 2, may hold values from -16 to 16
- error: bfloat16 [16, 4096, 6144], P('dp', None, 'expert'), parts along dimension 2, may hold values from -6 to 6
- q_start: float32 [6144, 32], P('expert'), parts along dimension 0, may hold values from -6 to 6
- bucket: float32 [16, 524288], P('dp', 'expert'), parts along dimension 1, may hold values from -6 to 6
Outputs:
- update: float32 [4096, 6144], P(None, 'expert'), parts along dimension 1
- new_error: bfloat16 [16, 4096, 6144], P('dp', None, 'expert'), parts along dimension 2
- bucket_mean: float32 [524288], P(('expert', 'dp')), parts along dimension 0
The draws below stay inside these ranges and needn't reach their ends.
There are 8 independent parts, one for each index of `expert`. The reference program is written for one: setup_inputs(seed, part) draws one part's arguments, and reference() takes and returns one part's arrays. A program takes and returns all parts, laid end to end along the dimension named above; each array names one. Nothing has to cross between parts.
All inputs are finite; a program needn't handle non-finite values.
Results may differ from the reference program's by a relative error of at most 0.02.
Values may be sent and summed in bfloat16 or wider, within the bound.
A program may use at most 128 MiB of HBM per device.

```python
import jax
import jax.numpy as jnp
from jax import lax

D = 4096
H = 768
R = 32
ITERS = 2
BUCKET = 65536
REPLICAS = 16
N_DP = 16


def raised(values, key, source, target, parts, factor):
    owner, partner = [(jnp.arange(values.shape[axis_at]) // (values.shape[axis_at] // parts)).reshape([-1 if axis == axis_at else 1 for axis in range(values.ndim)]) for axis_at in (source, target)]
    chosen = jax.random.permutation(key, parts)[partner]
    strong = (owner == chosen) | (owner == (partner + parts // 2) % parts)
    return jnp.where(strong, factor * values, values)


def block_scale(stream_key, dims, split, low, top_value):
    factor_of, own = 1.0, jax.random.fold_in(stream_key, 6)
    for position, shards_of in split:
        heights = jnp.exp(jax.random.uniform(jax.random.fold_in(own, position), (shards_of,), jnp.float32, low / len(split), top_value / len(split)))
        factor_of = factor_of * jnp.repeat(heights, dims[position] // shards_of).reshape([-1 if axis == position else 1 for axis in range(len(dims))])
    return factor_of


def gaussian(rng, extent, scale, bound, cuts=(), held_as=jnp.bfloat16):
    values = scale * jax.random.normal(rng, extent, jnp.float32)
    if cuts:
        values = values * block_scale(rng, extent, cuts, -0.22, 0.18)
    return jnp.clip(values, -bound, bound).astype(held_as)


def heavy_noise(key, extent, scale, most, cuts, heavy, kind=jnp.bfloat16):
    drawn = scale * jax.random.normal(key, extent, jnp.float32)
    if cuts:
        drawn = drawn * block_scale(key, extent, cuts, -0.22, 0.18)
    return jnp.clip(raised(drawn, jax.random.fold_in(key, 3), *heavy), -most, most).astype(kind)


def setup_inputs(seed: int = 0, part: int = 0) -> dict:
    key_list = jax.random.split(jax.random.key(seed), 5)
    own_keys = jax.random.split(jax.random.fold_in(key_list[4], part), 5)
    return {
        "grads": gaussian(own_keys[0], (REPLICAS, D, H), 4.0, 16.0, ((0, 16),)),
        "error": gaussian(own_keys[1], (REPLICAS, D, H), 1.0, 6.0, ((0, 16),)),
        "q_start": gaussian(own_keys[2], (H, R), 1.0, 6.0, (), jnp.float32),
        "bucket": heavy_noise(own_keys[3], (REPLICAS, BUCKET), 1.0, 6.0, ((0, 16),), (0, 1, 16, 2.0), jnp.float32),
    }


def reference(grads, error, q_start, bucket):
    compensated = (grads.astype(jnp.float32) + error.astype(jnp.float32)).astype(jnp.bfloat16)
    whole = compensated.astype(jnp.float32)
    factor_q = q_start
    p_half = None
    for step in range(ITERS):
        q_half = factor_q.astype(jnp.bfloat16).astype(jnp.float32)
        factor_p = jnp.einsum('rdh,hk->dk', whole, q_half) / N_DP
        gram = jnp.dot(factor_p.T, factor_p, precision=lax.Precision.HIGHEST)
        lower = jnp.linalg.cholesky(gram)
        p_hat = jax.scipy.linalg.solve_triangular(lower, factor_p.T, lower=True).T
        p_half = p_hat.astype(jnp.bfloat16).astype(jnp.float32)
        factor_q = jnp.einsum('rdh,dk->hk', whole, p_half) / N_DP
        if step + 1 < ITERS:
            factor_q = factor_q / jnp.sqrt(lax.optimization_barrier(jnp.sum(factor_q * factor_q, axis=0, keepdims=True)) + 1e-06)
    update = jnp.dot(p_half, factor_q.T, precision=lax.Precision.HIGHEST)
    new_error = (whole - update[None]).astype(jnp.bfloat16)
    bucket_mean = lax.optimization_barrier(jnp.sum(bucket, axis=0)) / N_DP
    return (update, new_error, bucket_mean)
```

```python
import functools

import jax
import jax.numpy as jnp
from jax import lax
from jax.experimental import pallas as pl
from jax.experimental.pallas import tpu as pltpu
from jax.sharding import PartitionSpec as P

ITERS = 2
MESH = pl.DeviceIdType.MESH
F32 = jnp.float32
BF16 = jnp.bfloat16


def offsets(side):
    near = lambda d: min(d, side - d)
    every = [(dz, dx) for dz in range(side) for dx in range(side) if (dz, dx) != (0, 0)]
    return sorted(every, key=lambda o: (-(near(o[0]) + near(o[1])), o))


def split3(x):
    hi = x.astype(BF16)
    rest = x - hi.astype(F32)
    mid = rest.astype(BF16)
    low = (rest - mid.astype(F32)).astype(BF16)
    return hi, mid, low


def inverse_cholesky(gram):
    n = gram.shape[0]
    lanes = 128
    row_id = lax.broadcasted_iota(jnp.int32, (n, lanes), 0)
    lane_id = lax.broadcasted_iota(jnp.int32, (n, lanes), 1)
    eye = (lane_id == row_id + n).astype(F32)
    work = jnp.concatenate([gram, jnp.zeros((n, lanes - n), F32)], axis=1) + eye
    out = jnp.zeros((n, lanes), F32)
    for k in range(n):
        row = work[k : k + 1, :]
        pivot = jnp.broadcast_to(row[:, k : k + 1], (1, lanes))
        out = jnp.where(row_id == k, row / jnp.sqrt(pivot), out)
        if k + 1 < n:
            column = jnp.broadcast_to(work[:, k : k + 1], (n, lanes))
            column = jnp.where(row_id > k, column, 0.0)
            work = work - column * (row / pivot)
    return out[:, n : 2 * n]


def iterate_kernel(
    n,
    side,
    grads,
    error,
    q_start,
    bucket,
    comp,
    p_out,
    q_out,
    mean_out,
    g_buf,
    e_buf,
    p_send,
    p_recv,
    p_all,
    q_x,
    b_buf,
    b_recv,
    load_sem,
    b_send_sem,
    b_recv_sem,
    rs_send_sem,
    rs_recv_sem,
    ag_send_sem,
    ag_recv_sem,
    q_send_sem,
    q_recv_sem,
):
    me = lax.axis_index("dp")
    my_z, my_x = lax.div(me, side), lax.rem(me, side)
    order = offsets(side)
    peers = [lax.rem(my_z + dz, side) * side + lax.rem(my_x + dx, side) for dz, dx in order]
    rows = comp.shape[1]
    rank = q_start.shape[0]
    inv_n = 1.0 / n

    def remote(src, dst, send, recv, peer):
        return pltpu.make_async_remote_copy(
            src_ref=src, dst_ref=dst, send_sem=send, recv_sem=recv, device_id={"dp": peer}, device_id_type=MESH
        )

    barrier = pltpu.get_barrier_semaphore()
    for peer in peers:
        pl.semaphore_signal(barrier, inc=1, device_id={"dp": peer}, device_id_type=MESH)

    def loads(j):
        part = pl.ds(pl.multiple_of(j * rows, rows), rows)
        return (
            pltpu.make_async_copy(grads.at[part], g_buf.at[j], load_sem.at[0, j]),
            pltpu.make_async_copy(error.at[part], e_buf.at[j], load_sem.at[1, j]),
        )

    for j in peers + [me]:
        for copy in loads(j):
            copy.start()

    b_buf[...] = bucket[...].astype(BF16)
    pl.semaphore_wait(barrier, n - 1)

    for peer in peers:
        remote(b_buf.at[peer], b_recv.at[me], b_send_sem.at[peer], b_recv_sem.at[me], peer).start()

    q_half = q_start[...].astype(BF16)
    for it in range(ITERS):
        def block(j):
            if it == 0:
                for copy in loads(j):
                    copy.wait()
                comp[j] = (g_buf[j].astype(F32) + e_buf[j].astype(F32)).astype(BF16)
            return lax.dot_general(q_half, comp[j], (((1,), (1,)), ((), ())), preferred_element_type=F32)

        for peer in peers:
            p_send[it, peer] = block(peer).astype(BF16)
            remote(
                p_send.at[it, peer],
                p_recv.at[it, me],
                rs_send_sem.at[it, peer],
                rs_recv_sem.at[it, me],
                peer,
            ).start()
        total = block(me)
        for peer in reversed(peers):
            remote(
                p_send.at[it, peer], p_recv.at[it, peer], rs_send_sem.at[it, peer], rs_recv_sem.at[it, peer], peer
            ).wait_recv()
            total = total + p_recv[it, peer].astype(F32)

        def mine(j):
            return p_all.at[it, :, pl.ds(pl.multiple_of(j * rows, rows), rows)]

        p_all[it, :, pl.ds(pl.multiple_of(me * rows, rows), rows)] = (total * inv_n).astype(BF16)
        for peer in peers:
            remote(mine(me), mine(me), ag_send_sem.at[it, peer], ag_recv_sem.at[it, me], peer).start()
        for peer in reversed(peers):
            remote(mine(me), mine(peer), ag_send_sem.at[it, peer], ag_recv_sem.at[it, peer], peer).wait_recv()

        factor_p = p_all[it]
        gram = lax.dot_general(factor_p, factor_p, (((1,), (1,)), ((), ())), preferred_element_type=F32)
        hi, mid, low = split3(inverse_cholesky(gram))
        p_hat = (
            jnp.dot(hi, factor_p, preferred_element_type=F32)
            + jnp.dot(mid, factor_p, preferred_element_type=F32)
            + jnp.dot(low, factor_p, preferred_element_type=F32)
        ).astype(BF16)

        local_q = jnp.zeros((rank, comp.shape[2]), F32)
        for j in range(n):
            local_q = local_q + jnp.dot(
                p_hat[:, j * rows : (j + 1) * rows], comp[j], preferred_element_type=F32
            )
        half = comp.shape[2] // 2
        parts = [local_q[:, :half], local_q[:, half:]]
        for stage in range(2):
            started = []
            for h in range(2):
                along_x = (h + stage) % 2 == 0
                mine_at = my_x if along_x else my_z
                q_x[it, stage, h, mine_at] = parts[h].astype(BF16)
                for d in (2, 1, 3):
                    at = lax.rem(mine_at + d, side)
                    peer = my_z * side + at if along_x else at * side + my_x
                    send = q_send_sem.at[it, stage, h, d]
                    slot = q_x.at[it, stage, h, mine_at]
                    remote(slot, slot, send, q_recv_sem.at[it, stage, h, mine_at], peer).start()
                    started.append((slot, q_x.at[it, stage, h, at], send, q_recv_sem.at[it, stage, h, at], peer))
            for args in started:
                remote(*args).wait_recv()
            for h in range(2):
                parts[h] = sum(q_x[it, stage, h, s].astype(F32) for s in range(side))
            for args in started:
                remote(*args).wait_send()
        factor_q = jnp.concatenate(parts, axis=1) * inv_n

        for peer in peers:
            remote(
                p_send.at[it, peer], p_recv.at[it, peer], rs_send_sem.at[it, peer], rs_recv_sem.at[it, peer], peer
            ).wait_send()
            remote(mine(me), mine(peer), ag_send_sem.at[it, peer], ag_recv_sem.at[it, peer], peer).wait_send()
        if it + 1 < ITERS:
            factor_q = factor_q / jnp.sqrt(jnp.sum(factor_q * factor_q, axis=1, keepdims=True) + 1e-06)
            q_half = factor_q.astype(BF16)
        else:
            p_out[...] = p_hat
            q_out[...] = factor_q

    share = b_buf[me].astype(F32)
    for peer in peers:
        copy = remote(b_buf.at[peer], b_recv.at[peer], b_send_sem.at[peer], b_recv_sem.at[peer], peer)
        copy.wait_recv()
        share = share + b_recv[peer].astype(F32)
        copy.wait_send()
    mean_out[...] = share * inv_n


def output_kernel(comp, p_hat, factor_q, update, new_error, u_buf, n_buf, sem):
    blocks, rows, _ = comp.shape
    hi, mid, low = split3(factor_q[...])
    right = jnp.concatenate([hi, mid, low], axis=0)

    def stores(j):
        slot = j % 2
        part = pl.ds(j * rows, rows)
        return (
            pltpu.make_async_copy(u_buf.at[slot], update.at[part], sem.at[0, slot]),
            pltpu.make_async_copy(n_buf.at[slot], new_error.at[part], sem.at[1, slot]),
        )

    for j in range(blocks):
        slot = j % 2
        if j >= 2:
            for copy in stores(j - 2):
                copy.wait()
        left = p_hat[:, j * rows : (j + 1) * rows]
        left = jnp.concatenate([left, left, left], axis=0)
        value = lax.dot_general(left, right, (((0,), (0,)), ((), ())), preferred_element_type=F32)
        u_buf[slot] = value
        n_buf[slot] = (comp[j].astype(F32) - value).astype(BF16)
        for copy in stores(j):
            copy.start()
    for j in (blocks - 2, blocks - 1):
        for copy in stores(j):
            copy.wait()


def on_device(n, side, grads, error, q_start, bucket):
    depth, width = grads.shape[1:]
    rank = q_start.shape[1]
    rows = depth // n
    shares = bucket.shape[1] // n // 128
    vmem = pl.BlockSpec(memory_space=pltpu.VMEM)
    anywhere = pl.BlockSpec(memory_space=pltpu.HBM)
    sds = jax.ShapeDtypeStruct
    dma = pltpu.SemaphoreType.DMA
    comp, p_hat, factor_q, mean = pl.pallas_call(
        functools.partial(iterate_kernel, n, side),
        out_shape=(
            sds((n, rows, width), BF16),
            sds((rank, depth), BF16),
            sds((rank, width), F32),
            sds((shares, 128), F32),
        ),
        in_specs=[anywhere, anywhere, vmem, vmem],
        out_specs=(vmem, vmem, vmem, vmem),
        scratch_shapes=[
            pltpu.VMEM((n, rows, width), BF16),
            pltpu.VMEM((n, rows, width), BF16),
            pltpu.VMEM((ITERS, n, rank, rows), BF16),
            pltpu.VMEM((ITERS, n, rank, rows), BF16),
            pltpu.VMEM((ITERS, rank, depth), BF16),
            pltpu.VMEM((ITERS, 2, 2, side, rank, width // 2), BF16),
            pltpu.VMEM((n, shares, 128), BF16),
            pltpu.VMEM((n, shares, 128), BF16),
            dma((2, n)),
            dma((n,)),
            dma((n,)),
            dma((ITERS, n)),
            dma((ITERS, n)),
            dma((ITERS, n)),
            dma((ITERS, n)),
            dma((ITERS, 2, 2, side)),
            dma((ITERS, 2, 2, side)),
        ],
        compiler_params=pltpu.CompilerParams(
            collective_id=0, has_side_effects=True, vmem_limit_bytes=40 << 20
        ),
        name="iterate",
    )(grads[0], error[0], q_start.T, bucket.reshape(n, shares, 128))

    update, new_error = pl.pallas_call(
        output_kernel,
        out_shape=(sds((depth, width), F32), sds((depth, width), BF16)),
        in_specs=[vmem, vmem, vmem],
        out_specs=(anywhere, anywhere),
        scratch_shapes=[
            pltpu.VMEM((2, rows, width), F32),
            pltpu.VMEM((2, rows, width), BF16),
            dma((2, 2)),
        ],
        compiler_params=pltpu.CompilerParams(vmem_limit_bytes=16 << 20),
        name="outputs",
    )(comp, p_hat, factor_q)
    return update, new_error[None], mean.reshape(-1)


def solution(mesh):
    n = mesh.shape["dp"]
    side = next(s for s in range(1, n + 1) if s * s == n)
    return jax.shard_map(
        functools.partial(on_device, n, side),
        mesh=mesh,
        in_specs=(
            P("dp", None, "expert"),
            P("dp", None, "expert"),
            P("expert", None),
            P("dp", "expert"),
        ),
        out_specs=(P(None, "expert"), P("dp", None, "expert"), P(("expert", "dp"))),
        check_vma=False,
    )
```

```python
import contextlib
import functools

import jax
import jax.numpy as jnp
from jax import lax
from jax.experimental import pallas as pl
from jax.experimental.pallas import tpu as pltpu
from jax.sharding import PartitionSpec as P

ITERS = 2
MESH = pl.DeviceIdType.MESH
F32 = jnp.float32
BF16 = jnp.bfloat16
AHEAD = 6
TRACE = False


def scope(name):
    return jax.named_scope(name) if TRACE else contextlib.nullcontext()


def runs(items, sizes):
    out = []
    for size in sizes:
        out.append(items[:size])
        items = items[size:]
    assert not items
    return out


def offsets(side):
    near = lambda d: min(d, side - d)
    every = [(dz, dx) for dz in range(side) for dx in range(side) if (dz, dx) != (0, 0)]
    return sorted(every, key=lambda o: (-(near(o[0]) + near(o[1])), o))


def split3(x):
    hi = x.astype(BF16)
    rest = x - hi.astype(F32)
    mid = rest.astype(BF16)
    low = (rest - mid.astype(F32)).astype(BF16)
    return hi, mid, low


def inverse_cholesky(gram, block=8):
    n, lanes, tile = gram.shape[0], 128, 8
    row_id = lax.broadcasted_iota(jnp.int32, (n, lanes), 0)
    lane_id = lax.broadcasted_iota(jnp.int32, (n, lanes), 1)
    eye = (lane_id == row_id + n).astype(F32)
    work = jnp.concatenate([gram, jnp.zeros((n, lanes - n), F32)], axis=1) + eye
    work = [work[tile * i : tile * (i + 1)] for i in range(n // tile)]
    out = [jnp.zeros((tile, lanes), F32) for _ in work]
    tile_row = row_id[:tile]
    for s in range(0, n, block):
        rows = [work[k // tile][k % tile : k % tile + 1] for k in range(s, s + block)]
        pivots = [
            [jnp.broadcast_to(rows[i][:, s + j : s + j + 1], (1, lanes)) for j in range(i + 1)] for i in range(block)
        ]
        rest = range((s + block) // tile, n // tile)
        columns = {
            (t, i): jnp.broadcast_to(work[t][:, s + i : s + i + 1], (tile, lanes)) for t in rest for i in range(block)
        }
        factor, inverse = {}, []
        for p in range(block):
            inverse.append(1.0 / pivots[p][p])
            for i in range(p + 1, block):
                factor[i, p] = pivots[i][p] * inverse[p]
                for j in range(p + 1, i + 1):
                    pivots[i][j] = pivots[i][j] - factor[i, p] * pivots[j][p]
                rows[i] = rows[i] - factor[i, p] * rows[p]
        for p in range(block):
            t, at = divmod(s + p, tile)
            out[t] = jnp.where(tile_row == at, rows[p] / jnp.sqrt(pivots[p][p]), out[t])
        solved = [rows[p] * inverse[p] for p in range(block)]
        for p in reversed(range(block)):
            for i in range(p + 1, block):
                solved[p] = solved[p] - factor[i, p] * solved[i]
        for t in rest:
            for i in range(block):
                work[t] = work[t] - columns[t, i] * solved[i]
    return jnp.concatenate(out, axis=0)[:, n : 2 * n]


def iterate_kernel(
    n,
    side,
    grads,
    error,
    q_start,
    bucket,
    comp,
    p_out,
    q_out,
    mean_out,
    comp_t,
    g_buf,
    e_buf,
    p_send,
    p_recv,
    p_all,
    q_x,
    q0_buf,
    b0_buf,
    b_buf,
    b_recv,
    load_sem,
    small_sem,
    b_send_sem,
    b_recv_sem,
    rs_send_sem,
    rs_recv_sem,
    ag_send_sem,
    ag_recv_sem,
    q_send_sem,
    q_recv_sem,
):
    me = lax.axis_index("dp")
    my_z, my_x = lax.div(me, side), lax.rem(me, side)
    order = offsets(side)
    peers = [lax.rem(my_z + dz, side) * side + lax.rem(my_x + dx, side) for dz, dx in order]
    rows = comp.shape[1]
    rank = q_start.shape[0]
    inv_n = 1.0 / n

    def remote(src, dst, send, recv, peer):
        return pltpu.make_async_remote_copy(
            src_ref=src, dst_ref=dst, send_sem=send, recv_sem=recv, device_id={"dp": peer}, device_id_type=MESH
        )

    barrier = pltpu.get_barrier_semaphore()
    for peer in peers:
        pl.semaphore_signal(barrier, inc=1, device_id={"dp": peer}, device_id_type=MESH)

    def loads(j):
        part = pl.ds(pl.multiple_of(j * rows, rows), rows)
        return (
            pltpu.make_async_copy(grads.at[part], g_buf.at[j], load_sem.at[0, j]),
            pltpu.make_async_copy(error.at[part], e_buf.at[j], load_sem.at[1, j]),
        )

    every = peers + [me]
    small = (
        pltpu.make_async_copy(q_start, q0_buf, small_sem.at[0]),
        pltpu.make_async_copy(bucket, b0_buf, small_sem.at[1]),
    )
    with scope("issue"):
        for j in every[:AHEAD]:
            for copy in loads(j):
                copy.start()
            if j is every[0]:
                small[0].start()
    def rs_copy(it, peer, slot):
        return remote(
            p_send.at[it, peer], p_recv.at[it, slot], rs_send_sem.at[it, peer], rs_recv_sem.at[it, slot], peer
        )

    def ag_copy(it, peer, slot):
        return remote(p_all.at[it, me], p_all.at[it, slot], ag_send_sem.at[it, peer], ag_recv_sem.at[it, slot], peer)

    def bucket_copy(peer, slot):
        return remote(b_buf.at[peer], b_recv.at[slot], b_send_sem.at[peer], b_recv_sem.at[slot], peer)

    for it in range(ITERS):
        with scope(f"p_local{it}"):
            loaded = 0
            for at, run in enumerate(runs(every, (1, 2, 3, 3, 3, 3, 1) if it == 0 else (5, 6, 5))):
                if it == 0:
                    with scope("load"):
                        for j in run:
                            for copy in loads(j):
                                copy.wait()
                        loaded += len(run)
                        for j in every[AHEAD + loaded - len(run) : AHEAD + loaded]:
                            for copy in loads(j):
                                copy.start()
                    for j in run:
                        comp[j] = g_buf[j] + e_buf[j]
                        comp_t[j] = comp[j].T
                    if at == 0:
                        small[0].wait()
                        q_half = q0_buf[...].astype(BF16)
                blocks = [jnp.dot(q_half, comp_t[j], preferred_element_type=F32) for j in run]
                for j, part in zip(run, blocks):
                    if j is me:
                        total = part
                    else:
                        p_send[it, j] = part.astype(BF16)
                if it > 0 or at > 1:
                    for j in run:
                        if j is not me:
                            rs_copy(it, j, me).start()
                elif at == 1:
                    with scope("entry"):
                        pl.semaphore_wait(barrier, n - 1)
                    for j in every[:loaded]:
                        rs_copy(it, j, me).start()
                    small[1].start()
        if it == ITERS - 1:
            with scope("bucket"):
                for peer in peers:
                    bucket_copy(peer, peer).wait_recv()
                share = b_buf[me].astype(F32)
                for peer in peers:
                    share = share + b_recv[peer].astype(F32)
                mean_out[...] = share * inv_n
        with scope(f"rs{it}"):
            for run in runs(peers[::-1], (10, 5)):
                for peer in run:
                    rs_copy(it, peer, peer).wait_recv()
                for peer in run:
                    total = total + p_recv[it, peer].astype(F32)
            p_all[it, me] = (total * inv_n).astype(BF16)

        with scope(f"ag{it}"):
            for peer in peers:
                ag_copy(it, peer, me).start()
            gram = jnp.zeros((rank, rank), F32)
            raw_q = jnp.zeros((rank, comp.shape[2]), F32)
            for run in runs(every[::-1], (5, 6, 4, 1)):
                for j in run:
                    if j is not me:
                        ag_copy(it, j, j).wait_recv()
                for j in run:
                    part = p_all[it, j]
                    gram = gram + lax.dot_general(part, part, (((1,), (1,)), ((), ())), preferred_element_type=F32)
                    raw_q = raw_q + jnp.dot(part, comp[j], preferred_element_type=F32)
        if it == 0:
            with scope("bucket"):
                small[1].wait()
                b_buf[...] = b0_buf[...].astype(BF16)
                for peer in peers:
                    bucket_copy(peer, me).start()
        with scope(f"cholesky{it}"):
            inverse = inverse_cholesky(gram)

        half = comp.shape[2] // 2
        for stage in range(2):
            with scope(f"q_send{it}_{stage}"):
                started = []
                for h in range(2):
                    if stage == 0:
                        part = jnp.dot(
                            inverse,
                            raw_q[:, h * half : (h + 1) * half],
                            preferred_element_type=F32,
                            precision=lax.Precision.HIGHEST,
                        )
                    else:
                        part = parts[h]
                    along_x = (h + stage) % 2 == 0
                    mine_at = my_x if along_x else my_z
                    slot = q_x.at[it, stage, h, mine_at]
                    slot[...] = part.astype(BF16)
                    for d in (2, 1, 3):
                        at = lax.rem(mine_at + d, side)
                        peer = my_z * side + at if along_x else at * side + my_x
                        send = q_send_sem.at[it, stage, h, d]
                        remote(slot, slot, send, q_recv_sem.at[it, stage, h, mine_at], peer).start()
                        started.append((slot, q_x.at[it, stage, h, at], send, q_recv_sem.at[it, stage, h, at], peer))
            if stage == 0 and it == ITERS - 1:
                with scope("p_hat"):
                    pieces = split3(inverse)
                    for j in range(n):
                        p_out[:, j * rows : (j + 1) * rows] = sum(
                            jnp.dot(piece, p_all[it, j], preferred_element_type=F32) for piece in pieces
                        ).astype(BF16)
            with scope(f"q_wait{it}_{stage}"):
                for args in started:
                    remote(*args).wait_recv()
            parts = [sum(q_x[it, stage, h, s].astype(F32) for s in range(side)) for h in range(2)]
            for args in started:
                remote(*args).wait_send()
        factor_q = jnp.concatenate(parts, axis=1) * inv_n
        if it + 1 < ITERS:
            factor_q = factor_q / jnp.sqrt(jnp.sum(factor_q * factor_q, axis=1, keepdims=True) + 1e-06)
            q_half = factor_q.astype(BF16)
        else:
            q_out[...] = factor_q

    with scope("sends"):
        for peer in peers:
            for it in range(ITERS):
                rs_copy(it, peer, peer).wait_send()
                ag_copy(it, peer, peer).wait_send()
            bucket_copy(peer, peer).wait_send()


def output_kernel(comp, p_hat, factor_q, mean, update, new_error, mean_out, u_buf, n_buf, sem, mean_sem):
    blocks, rows, _ = comp.shape
    mean_copy = pltpu.make_async_copy(mean, mean_out, mean_sem)
    mean_copy.start()
    hi, mid, low = split3(factor_q[...])
    right = jnp.concatenate([hi, mid, low], axis=0)

    slots = u_buf.shape[0]

    def stores(j):
        slot = j % slots
        part = pl.ds(j * rows, rows)
        return (
            pltpu.make_async_copy(u_buf.at[slot], update.at[part], sem.at[0, slot]),
            pltpu.make_async_copy(n_buf.at[slot], new_error.at[part], sem.at[1, slot]),
        )

    for j in range(blocks):
        slot = j % slots
        if j >= slots:
            with scope("stores"):
                for copy in stores(j - slots):
                    copy.wait()
        with scope("block"):
            left = p_hat[:, j * rows : (j + 1) * rows]
            left = jnp.concatenate([left, left, left], axis=0)
            value = lax.dot_general(left, right, (((0,), (0,)), ((), ())), preferred_element_type=F32)
            u_buf[slot] = value
            n_buf[slot] = (comp[j].astype(F32) - value).astype(BF16)
        for copy in stores(j):
            copy.start()
    with scope("last"):
        for j in range(blocks - slots, blocks):
            for copy in stores(j):
                copy.wait()
    mean_copy.wait()


def in_hbm(array):
    return pltpu.with_memory_space_constraint(array, pltpu.HBM)


def on_device(n, side, grads, error, q_start, bucket):
    depth, width = grads.shape[1:]
    rank = q_start.shape[1]
    rows = depth // n
    shares = bucket.shape[1] // n // 128
    vmem = pl.BlockSpec(memory_space=pltpu.VMEM)
    anywhere = pl.BlockSpec(memory_space=pltpu.HBM)
    sds = jax.ShapeDtypeStruct
    dma = pltpu.SemaphoreType.DMA
    comp, p_hat, factor_q, mean = pl.pallas_call(
        functools.partial(iterate_kernel, n, side),
        out_shape=(
            sds((n, rows, width), BF16),
            sds((rank, depth), BF16),
            sds((rank, width), F32),
            sds((shares, 128), F32),
        ),
        in_specs=[anywhere] * 4,
        out_specs=(vmem, vmem, vmem, vmem),
        scratch_shapes=[
            pltpu.VMEM((n, width, rows), BF16),
            pltpu.VMEM((n, rows, width), BF16),
            pltpu.VMEM((n, rows, width), BF16),
            pltpu.VMEM((ITERS, n, rank, rows), BF16),
            pltpu.VMEM((ITERS, n, rank, rows), BF16),
            pltpu.VMEM((ITERS, n, rank, rows), BF16),
            pltpu.VMEM((ITERS, 2, 2, side, rank, width // 2), BF16),
            pltpu.VMEM((rank, width), F32),
            pltpu.VMEM((n, shares, 128), F32),
            pltpu.VMEM((n, shares, 128), BF16),
            pltpu.VMEM((n, shares, 128), BF16),
            dma((2, n)),
            dma((2,)),
            dma((n,)),
            dma((n,)),
            dma((ITERS, n)),
            dma((ITERS, n)),
            dma((ITERS, n)),
            dma((ITERS, n)),
            dma((ITERS, 2, 2, side)),
            dma((ITERS, 2, 2, side)),
        ],
        compiler_params=pltpu.CompilerParams(
            collective_id=0, has_side_effects=True, vmem_limit_bytes=40 << 20
        ),
        name="iterate",
    )(*(in_hbm(a) for a in (grads[0], error[0], q_start.T, bucket.reshape(n, shares, 128))))

    update, new_error, mean = pl.pallas_call(
        output_kernel,
        out_shape=(sds((depth, width), F32), sds((depth, width), BF16), sds((shares, 128), F32)),
        in_specs=[vmem, vmem, vmem, vmem],
        out_specs=(anywhere, anywhere, anywhere),
        scratch_shapes=[
            pltpu.VMEM((4, rows, width), F32),
            pltpu.VMEM((4, rows, width), BF16),
            dma((2, 4)),
            dma,
        ],
        compiler_params=pltpu.CompilerParams(vmem_limit_bytes=16 << 20),
        name="outputs",
    )(comp, p_hat, factor_q, mean)
    return update, new_error[None], mean.reshape(-1)


def solution(mesh):
    n = mesh.shape["dp"]
    side = next(s for s in range(1, n + 1) if s * s == n)
    return jax.shard_map(
        functools.partial(on_device, n, side),
        mesh=mesh,
        in_specs=(
            P("dp", None, "expert"),
            P("dp", None, "expert"),
            P("expert", None),
            P("dp", "expert"),
        ),
        out_specs=(P(None, "expert"), P("dp", None, "expert"), P(("expert", "dp"))),
        check_vma=False,
    )
```

```python
import contextlib
import functools

import jax
import jax.numpy as jnp
from jax import lax
from jax.experimental import pallas as pl
from jax.experimental.pallas import tpu as pltpu
from jax.sharding import PartitionSpec as P

ITERS = 2
MESH = pl.DeviceIdType.MESH
F32 = jnp.float32
BF16 = jnp.bfloat16
AHEAD = 6
FIRST_RUNS = (1, 2, 3, 3, 3, 3, 1)
LATER_RUNS = (5, 6, 5)
BARRIER_RUN = 3
TRACE = False


def scope(name):
    return jax.named_scope(name) if TRACE else contextlib.nullcontext()


def runs(items, sizes):
    out = []
    for size in sizes:
        out.append(items[:size])
        items = items[size:]
    assert not items
    return out


def offsets(side):
    near = lambda d: min(d, side - d)
    every = [(dz, dx) for dz in range(side) for dx in range(side) if (dz, dx) != (0, 0)]
    return sorted(every, key=lambda o: (-(near(o[0]) + near(o[1])), o))


def split3(x):
    hi = x.astype(BF16)
    rest = x - hi.astype(F32)
    mid = rest.astype(BF16)
    low = (rest - mid.astype(F32)).astype(BF16)
    return hi, mid, low


def inverse_cholesky(gram, block=8):
    n, lanes, tile = gram.shape[0], 128, 8
    row_id = lax.broadcasted_iota(jnp.int32, (n, lanes), 0)
    lane_id = lax.broadcasted_iota(jnp.int32, (n, lanes), 1)
    eye = (lane_id == row_id + n).astype(F32)
    work = jnp.concatenate([gram, jnp.zeros((n, lanes - n), F32)], axis=1) + eye
    work = [work[tile * i : tile * (i + 1)] for i in range(n // tile)]
    out = [jnp.zeros((tile, lanes), F32) for _ in work]
    tile_row = row_id[:tile]
    for s in range(0, n, block):
        rows = [work[k // tile][k % tile : k % tile + 1] for k in range(s, s + block)]
        pivots = [
            [jnp.broadcast_to(rows[i][:, s + j : s + j + 1], (1, lanes)) for j in range(i + 1)] for i in range(block)
        ]
        rest = range((s + block) // tile, n // tile)
        columns = {
            (t, i): jnp.broadcast_to(work[t][:, s + i : s + i + 1], (tile, lanes)) for t in rest for i in range(block)
        }
        factor, inverse = {}, []
        for p in range(block):
            inverse.append(1.0 / pivots[p][p])
            for i in range(p + 1, block):
                factor[i, p] = pivots[i][p] * inverse[p]
                for j in range(p + 1, i + 1):
                    pivots[i][j] = pivots[i][j] - factor[i, p] * pivots[j][p]
                rows[i] = rows[i] - factor[i, p] * rows[p]
        for p in range(block):
            t, at = divmod(s + p, tile)
            out[t] = jnp.where(tile_row == at, rows[p] / jnp.sqrt(pivots[p][p]), out[t])
        solved = [rows[p] * inverse[p] for p in range(block)]
        for p in reversed(range(block)):
            for i in range(p + 1, block):
                solved[p] = solved[p] - factor[i, p] * solved[i]
        for t in rest:
            for i in range(block):
                work[t] = work[t] - columns[t, i] * solved[i]
    return jnp.concatenate(out, axis=0)[:, n : 2 * n]


def group_of(side):
    me = lax.axis_index("dp")
    my_z, my_x = lax.div(me, side), lax.rem(me, side)
    peers = [lax.rem(my_z + dz, side) * side + lax.rem(my_x + dx, side) for dz, dx in offsets(side)]
    return me, my_z, my_x, peers


def iterate_kernel(
    n,
    side,
    grads,
    error,
    q_start,
    bucket,
    comp,
    p_out,
    q_out,
    mean_out,
    comp_t,
    ge_buf,
    p_send,
    p_recv,
    p_all,
    q_x,
    q0_buf,
    b0_buf,
    b_buf,
    b_recv,
    load_sem,
    small_sem,
    send_sem,
    b_recv_sem,
    rs_recv_sem,
    ag_recv_sem,
    q_recv_sem,
):
    me, my_z, my_x, peers = group_of(side)
    every = peers + [me]
    own = n - 1
    order = offsets(side)
    back = [order.index(((side - dz) % side, (side - dx) % side)) for dz, dx in order]
    steps = [min(dz, side - dz) + min(dx, side - dx) for dz, dx in order]
    rings = [[i for i in range(own) if steps[i] == step] for step in sorted(set(steps), reverse=True)]
    ring_of = [next(r for r, ring in enumerate(rings) if i in ring) for i in range(own)]
    rows = comp.shape[1]
    rank = q_start.shape[0]
    inv_n = 1.0 / n

    def remote(src, dst, send, recv, peer):
        return pltpu.make_async_remote_copy(
            src_ref=src, dst_ref=dst, send_sem=send, recv_sem=recv, device_id={"dp": peer}, device_id_type=MESH
        )

    barrier = pltpu.get_barrier_semaphore()
    for peer in peers:
        pl.semaphore_signal(barrier, inc=1, device_id={"dp": peer}, device_id_type=MESH)

    first_runs = runs(list(range(n)), FIRST_RUNS)
    run_of = [next(r for r, run in enumerate(first_runs) if i in run) for i in range(n)]

    def load(i):
        part = pl.ds(pl.multiple_of(every[i] * rows, rows), rows)
        for k, source in enumerate((grads, error)):
            pltpu.make_async_copy(source.at[part], ge_buf.at[i, k], load_sem.at[run_of[i]]).start()

    def loaded(r):
        held = ge_buf.at[pl.ds(first_runs[r][0], len(first_runs[r]))]
        pltpu.make_async_copy(held, held, load_sem.at[r]).wait()

    small = (
        pltpu.make_async_copy(q_start, q0_buf, small_sem.at[0]),
        pltpu.make_async_copy(bucket, b0_buf, small_sem.at[1]),
    )
    for i in range(AHEAD):
        load(i)
        if i == 0:
            small[0].start()

    def rs_send(it, i):
        remote(
            p_send.at[it, i], p_recv.at[it, back[i]], send_sem.at[0], rs_recv_sem.at[it, ring_of[i]], peers[i]
        ).start()

    def rs_wait(it, r):
        held = p_recv.at[it, pl.ds(rings[r][0], len(rings[r]))]
        remote(held, held, send_sem.at[0], rs_recv_sem.at[it, r], peers[0]).wait_recv()

    def ag_send(it, i):
        held = p_all.at[it, me]
        remote(held, held, send_sem.at[1], ag_recv_sem.at[it, ring_of[i]], peers[i]).start()

    def ag_wait(it, r):
        held = p_all.at[it, pl.ds(0, len(rings[r]))]
        remote(held, held, send_sem.at[1], ag_recv_sem.at[it, r], peers[0]).wait_recv()

    for it in range(ITERS):
        def multiply(run):
            blocks = [jnp.dot(q_half, comp_t[i], preferred_element_type=F32) for i in run]
            for i, part in zip(run, blocks):
                if i != own:
                    p_send[it, i] = part.astype(BF16)
            return blocks[-1]

        def send(run):
            for i in run:
                if i != own:
                    rs_send(it, i)

        with scope(f"p_local{it}"):
            if it == 0:
                before, ready = [], []
                for r, run in enumerate(first_runs):
                    with scope("load"):
                        loaded(r)
                        for i in range(AHEAD + run[0], min(AHEAD + run[-1] + 1, n)):
                            load(i)
                        if r == 1:
                            small[0].wait()
                            q_half = q0_buf[...].astype(BF16)
                    for i in run:
                        comp[i] = ge_buf[i, 0] + ge_buf[i, 1]
                        comp_t[i] = comp[i].T
                    if before:
                        multiply(before)
                        ready = ready + before
                    before = run
                    if r == BARRIER_RUN:
                        small[1].start()
                        with scope("entry"):
                            pl.semaphore_wait(barrier, n - 1)
                    if r >= BARRIER_RUN:
                        send(ready)
                        ready = []
                total = multiply(before)
                send(before)
            else:
                for run in runs(list(range(n)), LATER_RUNS):
                    total = multiply(run)
                    send(run)
        if it == ITERS - 1:
            with scope("bucket"):
                remote(b_recv, b_recv, send_sem.at[2], b_recv_sem, peers[0]).wait_recv()
                share = b_buf[me].astype(F32)
                for i in range(own):
                    share = share + b_recv[i].astype(F32)
                mean_out[...] = share * inv_n
        with scope(f"rs{it}"):
            for r in reversed(range(len(rings))):
                rs_wait(it, r)
                for i in rings[r]:
                    total = total + p_recv[it, i].astype(F32)
            p_all[it, me] = (total * inv_n).astype(BF16)

        with scope(f"ag{it}"):
            for i in range(own):
                ag_send(it, i)
            raw_q = jnp.dot(p_all[it, me], comp[own], preferred_element_type=F32)
            for r in reversed(range(len(rings))):
                ag_wait(it, r)
                for i in rings[r]:
                    raw_q = raw_q + jnp.dot(p_all[it, peers[i]], comp[i], preferred_element_type=F32)
            gram = jnp.zeros((rank, rank), F32)
            for j in range(n):
                part = p_all[it, j]
                gram = gram + lax.dot_general(part, part, (((1,), (1,)), ((), ())), preferred_element_type=F32)
        if it == 0:
            with scope("bucket"):
                small[1].wait()
                b_buf[...] = b0_buf[...].astype(BF16)
                for i, peer in enumerate(peers):
                    remote(b_buf.at[peer], b_recv.at[back[i]], send_sem.at[2], b_recv_sem, peer).start()
        with scope(f"cholesky{it}"):
            inverse = inverse_cholesky(gram)

        half = comp.shape[2] // 2

        def q_start_half(stage, h, part):
            along_x = (h + stage) % 2 == 0
            mine_at = my_x if along_x else my_z
            slot = q_x.at[it, stage, h, mine_at]
            slot[...] = part.astype(BF16)
            for d in (2, 1, 3):
                at = lax.rem(mine_at + d, side)
                peer = my_z * side + at if along_x else at * side + my_x
                remote(slot, slot, send_sem.at[3], q_recv_sem.at[it, stage, h], peer).start()

        def q_sum_half(stage, h):
            with scope(f"q_wait{it}_{stage}"):
                held = q_x.at[it, stage, h, pl.ds(0, side - 1)]
                remote(held, held, send_sem.at[3], q_recv_sem.at[it, stage, h], peers[0]).wait_recv()
            return sum(q_x[it, stage, h, s].astype(F32) for s in range(side))

        with scope(f"q_send{it}"):
            for h in range(2):
                part = jnp.dot(
                    inverse,
                    raw_q[:, h * half : (h + 1) * half],
                    preferred_element_type=F32,
                    precision=lax.Precision.HIGHEST,
                )
                q_start_half(0, h, part)
        if it == ITERS - 1:
            with scope("p_hat"):
                pieces = split3(inverse)
                for i in range(n):
                    block = p_all[it, every[i]]
                    p_hat = sum(jnp.dot(piece, block, preferred_element_type=F32) for piece in pieces)
                    p_hat = p_hat.T.astype(BF16)
                    p_out[i] = jnp.concatenate([p_hat, p_hat, p_hat], axis=1)
        for h in range(2):
            q_start_half(1, h, q_sum_half(0, h))
        parts = [q_sum_half(1, h) for h in range(2)]
        factor_q = jnp.concatenate(parts, axis=1) * inv_n
        if it + 1 < ITERS:
            factor_q = factor_q / jnp.sqrt(jnp.sum(factor_q * factor_q, axis=1, keepdims=True) + 1e-06)
            q_half = factor_q.astype(BF16)
        else:
            q_out[...] = factor_q

    with scope("sends"):
        blocks = p_all.at[:, pl.ds(0, own)]
        shares = b_buf.at[pl.ds(0, own)]
        halves = q_x.at[:, :, :, pl.ds(0, side - 1)]
        for k, (held, arrived) in enumerate(
            (
                (p_send, rs_recv_sem.at[0, 0]),
                (blocks, ag_recv_sem.at[0, 0]),
                (shares, b_recv_sem),
                (halves, q_recv_sem.at[0, 0, 0]),
            )
        ):
            remote(held, held, send_sem.at[k], arrived, peers[0]).wait_send()


def output_kernel(
    side, comp, p_hat, factor_q, mean, update, new_error, mean_out, u_buf, n_buf, sem, mean_sem
):
    me, _, _, peers = group_of(side)
    every = peers + [me]
    n, rows, _ = comp.shape
    mean_copy = pltpu.make_async_copy(mean, mean_out, mean_sem)
    mean_copy.start()
    right = jnp.concatenate(split3(factor_q[...]), axis=0)
    slots = u_buf.shape[0]
    small = rows // 2
    steps = [[(0, 0, small)], [(0, small, small)], [(1, 0, rows)]]
    steps += [[(i, 0, rows), (i + 1, 0, rows)] for i in range(2, n, 2)]

    def stored(k):
        slot, size = k % slots, pl.ds(0, sum(piece[2] for piece in steps[k]))
        for which, held in enumerate((u_buf.at[slot, size], n_buf.at[slot, size])):
            pltpu.make_async_copy(held, held, sem.at[which, slot]).wait()

    for k, step in enumerate(steps):
        slot = k % slots
        if k >= slots:
            with scope("stores"):
                stored(k - slots)
        with scope("block"):
            at = 0
            for i, r, size in step:
                value = jnp.dot(p_hat[i, r : r + size], right, preferred_element_type=F32)
                u_buf[slot, at : at + size] = value
                n_buf[slot, at : at + size] = (comp[i, r : r + size].astype(F32) - value).astype(BF16)
                at += size
        at = 0
        for i, r, size in step:
            part = pl.ds(pl.multiple_of(every[i] * rows + r, size), size)
            held = pl.ds(at, size)
            pltpu.make_async_copy(u_buf.at[slot, held], update.at[part], sem.at[0, slot]).start()
            pltpu.make_async_copy(n_buf.at[slot, held], new_error.at[part], sem.at[1, slot]).start()
            at += size
    with scope("last"):
        for k in range(max(0, len(steps) - slots), len(steps)):
            stored(k)
    mean_copy.wait()


def in_hbm(array):
    return pltpu.with_memory_space_constraint(array, pltpu.HBM)


def on_device(n, side, grads, error, q_start, bucket):
    depth, width = grads.shape[1:]
    rank = q_start.shape[1]
    rows = depth // n
    shares = bucket.shape[1] // n // 128
    vmem = pl.BlockSpec(memory_space=pltpu.VMEM)
    anywhere = pl.BlockSpec(memory_space=pltpu.HBM)
    sds = jax.ShapeDtypeStruct
    dma = pltpu.SemaphoreType.DMA
    comp, p_hat, factor_q, mean = pl.pallas_call(
        functools.partial(iterate_kernel, n, side),
        out_shape=(
            sds((n, rows, width), BF16),
            sds((n, rows, 3 * rank), BF16),
            sds((rank, width), F32),
            sds((shares, 128), F32),
        ),
        in_specs=[anywhere] * 4,
        out_specs=(vmem, vmem, vmem, vmem),
        scratch_shapes=[
            pltpu.VMEM((n, width, rows), BF16),
            pltpu.VMEM((n, 2, rows, width), BF16),
            pltpu.VMEM((ITERS, n - 1, rank, rows), BF16),
            pltpu.VMEM((ITERS, n - 1, rank, rows), BF16),
            pltpu.VMEM((ITERS, n, rank, rows), BF16),
            pltpu.VMEM((ITERS, 2, 2, side, rank, width // 2), BF16),
            pltpu.VMEM((rank, width), F32),
            pltpu.VMEM((n, shares, 128), F32),
            pltpu.VMEM((n, shares, 128), BF16),
            pltpu.VMEM((n - 1, shares, 128), BF16),
            dma((len(FIRST_RUNS),)),
            dma((2,)),
            dma((4,)),
            dma,
            dma((ITERS, 4)),
            dma((ITERS, 4)),
            dma((ITERS, 2, 2)),
        ],
        compiler_params=pltpu.CompilerParams(
            collective_id=0, has_side_effects=True, vmem_limit_bytes=40 << 20
        ),
        name="iterate",
    )(*(in_hbm(a) for a in (grads[0], error[0], q_start.T, bucket.reshape(n, shares, 128))))

    update, new_error, mean = pl.pallas_call(
        functools.partial(output_kernel, side),
        out_shape=(sds((depth, width), F32), sds((depth, width), BF16), sds((shares, 128), F32)),
        in_specs=[vmem, vmem, vmem, vmem],
        out_specs=(anywhere, anywhere, anywhere),
        scratch_shapes=[
            pltpu.VMEM((4, 2 * rows, width), F32),
            pltpu.VMEM((4, 2 * rows, width), BF16),
            dma((2, 4)),
            dma,
        ],
        compiler_params=pltpu.CompilerParams(vmem_limit_bytes=16 << 20),
        name="outputs",
    )(comp, p_hat, factor_q, mean)
    return update, new_error[None], mean.reshape(-1)


def solution(mesh):
    n = mesh.shape["dp"]
    side = next(s for s in range(1, n + 1) if s * s == n)
    return jax.shard_map(
        functools.partial(on_device, n, side),
        mesh=mesh,
        in_specs=(
            P("dp", None, "expert"),
            P("dp", None, "expert"),
            P("expert", None),
            P("dp", "expert"),
        ),
        out_specs=(P(None, "expert"), P("dp", None, "expert"), P(("expert", "dp"))),
        check_vma=False,
    )
```

```python
import contextlib
import functools

import jax
import jax.numpy as jnp
from jax import lax
from jax.experimental import pallas as pl
from jax.experimental.pallas import tpu as pltpu
from jax.sharding import PartitionSpec as P

ITERS = 2
MESH = pl.DeviceIdType.MESH
F32 = jnp.float32
BF16 = jnp.bfloat16
AHEAD = 6
FIRST_RUNS = (2, 2, 2, 2, 2, 2, 2, 2)
LATER_RUNS = (5, 6, 5)
BARRIER_RUN = 3
TRACE = False


def scope(name):
    return jax.named_scope(name) if TRACE else contextlib.nullcontext()


def runs(items, sizes):
    out = []
    for size in sizes:
        out.append(items[:size])
        items = items[size:]
    assert not items
    return out


def offsets(side):
    near = lambda d: min(d, side - d)
    every = [(dz, dx) for dz in range(side) for dx in range(side) if (dz, dx) != (0, 0)]
    return sorted(every, key=lambda o: (-(near(o[0]) + near(o[1])), o))


def split3(x):
    hi = x.astype(BF16)
    rest = x - hi.astype(F32)
    mid = rest.astype(BF16)
    low = (rest - mid.astype(F32)).astype(BF16)
    return hi, mid, low


def inverse_cholesky(gram, block=8):
    n, lanes, tile = gram.shape[0], 128, 8
    row_id = lax.broadcasted_iota(jnp.int32, (n, lanes), 0)
    lane_id = lax.broadcasted_iota(jnp.int32, (n, lanes), 1)
    eye = ((lane_id >= n) & (lane_id % n == row_id)).astype(F32)
    work = jnp.concatenate([gram, jnp.zeros((n, lanes - n), F32)], axis=1) + eye
    work = [work[tile * i : tile * (i + 1)] for i in range(n // tile)]
    out = [jnp.zeros((tile, lanes), F32) for _ in work]
    tile_row = row_id[:tile]
    for s in range(0, n, block):
        rows = [work[k // tile][k % tile : k % tile + 1] for k in range(s, s + block)]
        pivots = [
            [jnp.broadcast_to(rows[i][:, s + j : s + j + 1], (1, lanes)) for j in range(i + 1)] for i in range(block)
        ]
        rest = range((s + block) // tile, n // tile)
        columns = {
            (t, i): jnp.broadcast_to(work[t][:, s + i : s + i + 1], (tile, lanes)) for t in rest for i in range(block)
        }
        factor, inverse = {}, []
        for p in range(block):
            inverse.append(1.0 / pivots[p][p])
            for i in range(p + 1, block):
                factor[i, p] = pivots[i][p] * inverse[p]
                for j in range(p + 1, i + 1):
                    pivots[i][j] = pivots[i][j] - factor[i, p] * pivots[j][p]
                rows[i] = rows[i] - factor[i, p] * rows[p]
        for p in range(block):
            t, at = divmod(s + p, tile)
            out[t] = jnp.where(tile_row == at, rows[p] / jnp.sqrt(pivots[p][p]), out[t])
        solved = [rows[p] * inverse[p] for p in range(block)]
        for p in reversed(range(block)):
            for i in range(p + 1, block):
                solved[p] = solved[p] - factor[i, p] * solved[i]
        for t in rest:
            for i in range(block):
                work[t] = work[t] - columns[t, i] * solved[i]
    return jnp.concatenate(out, axis=0)


def terms_in_lanes(inverse):
    n = inverse.shape[0]
    part = lax.broadcasted_iota(jnp.int32, inverse.shape, 1) // n
    hi, mid, low = (x.astype(F32) for x in split3(jnp.where(part == 0, 0.0, inverse)))
    start = jnp.where(part == 1, hi, jnp.where(part == 2, mid, 0.0))
    return jnp.where(part == 3, low, start).astype(BF16), jnp.where(part == 3, hi, start).astype(BF16)


def group_of(side):
    me = lax.axis_index("dp")
    my_z, my_x = lax.div(me, side), lax.rem(me, side)
    peers = [lax.rem(my_z + dz, side) * side + lax.rem(my_x + dx, side) for dz, dx in offsets(side)]
    return me, my_z, my_x, peers


def iterate_kernel(
    n,
    side,
    grads,
    error,
    q_start,
    bucket,
    comp,
    p_out,
    q_out,
    mean_out,
    comp_t,
    ge_buf,
    p_send,
    p_recv,
    p_all,
    q_x,
    q0_buf,
    b0_buf,
    b_buf,
    b_recv,
    load_sem,
    small_sem,
    send_sem,
    b_recv_sem,
    rs_recv_sem,
    ag_recv_sem,
    q_recv_sem,
):
    me, my_z, my_x, peers = group_of(side)
    every = peers + [me]
    own = n - 1
    order = offsets(side)
    back = [order.index(((side - dz) % side, (side - dx) % side)) for dz, dx in order]
    steps = [min(dz, side - dz) + min(dx, side - dx) for dz, dx in order]
    rings = [[i for i in range(own) if steps[i] == step] for step in sorted(set(steps), reverse=True)]
    ring_of = [next(r for r, ring in enumerate(rings) if i in ring) for i in range(own)]
    rows = comp.shape[1]
    rank = q_start.shape[0]
    inv_n = 1.0 / n

    def remote(src, dst, send, recv, peer):
        return pltpu.make_async_remote_copy(
            src_ref=src, dst_ref=dst, send_sem=send, recv_sem=recv, device_id={"dp": peer}, device_id_type=MESH
        )

    barrier = pltpu.get_barrier_semaphore()
    for peer in peers:
        pl.semaphore_signal(barrier, inc=1, device_id={"dp": peer}, device_id_type=MESH)

    first_runs = runs(list(range(n)), FIRST_RUNS)
    run_of = [next(r for r, run in enumerate(first_runs) if i in run) for i in range(n)]

    def load(i):
        part = pl.ds(pl.multiple_of(every[i] * rows, rows), rows)
        for k, source in enumerate((grads, error)):
            pltpu.make_async_copy(source.at[part], ge_buf.at[i, k], load_sem.at[run_of[i]]).start()

    def loaded(r):
        held = ge_buf.at[pl.ds(first_runs[r][0], len(first_runs[r]))]
        pltpu.make_async_copy(held, held, load_sem.at[r]).wait()

    small = (
        pltpu.make_async_copy(q_start, q0_buf, small_sem.at[0]),
        pltpu.make_async_copy(bucket, b0_buf, small_sem.at[1]),
    )
    for i in range(AHEAD):
        load(i)
        if i == 0:
            small[0].start()

    def rs_send(it, i):
        remote(
            p_send.at[it, i], p_recv.at[it, back[i]], send_sem.at[0], rs_recv_sem.at[it, ring_of[i]], peers[i]
        ).start()

    def rs_wait(it, r):
        held = p_recv.at[it, pl.ds(rings[r][0], len(rings[r]))]
        remote(held, held, send_sem.at[0], rs_recv_sem.at[it, r], peers[0]).wait_recv()

    def ag_send(it, i):
        held = p_all.at[it, me]
        remote(held, held, send_sem.at[1], ag_recv_sem.at[it, ring_of[i]], peers[i]).start()

    def ag_wait(it, r):
        held = p_all.at[it, pl.ds(0, len(rings[r]))]
        remote(held, held, send_sem.at[1], ag_recv_sem.at[it, r], peers[0]).wait_recv()

    for it in range(ITERS):
        def multiply(run):
            blocks = [jnp.dot(q_half, comp_t[i], preferred_element_type=F32) for i in run]
            for i, part in zip(run, blocks):
                if i != own:
                    p_send[it, i] = part.astype(BF16)
            return blocks[-1]

        def send(run):
            for i in run:
                if i != own:
                    rs_send(it, i)

        with scope(f"p_local{it}"):
            if it == 0:
                before, ready = [], []
                for r, run in enumerate(first_runs):
                    with scope("load"):
                        loaded(r)
                        for i in range(AHEAD + run[0], min(AHEAD + run[-1] + 1, n)):
                            load(i)
                        if r == 1:
                            small[0].wait()
                            q_half = q0_buf[...].astype(BF16)
                    for i in run:
                        comp[i] = ge_buf[i, 0] + ge_buf[i, 1]
                        comp_t[i] = comp[i].T
                    if before:
                        multiply(before)
                        ready = ready + before
                    before = run
                    if r == BARRIER_RUN:
                        with scope("entry"):
                            pl.semaphore_wait(barrier, n - 1)
                    if r >= BARRIER_RUN:
                        send(ready)
                        ready = []
                    if r == len(first_runs) - 2:
                        small[1].start()
                total = multiply(before)
                send(before)
            else:
                for run in runs(list(range(n)), LATER_RUNS):
                    total = multiply(run)
                    send(run)
        with scope(f"rs{it}"):
            for r in reversed(range(len(rings))):
                rs_wait(it, r)
                for i in rings[r]:
                    total = total + p_recv[it, i].astype(F32)
            p_all[it, me] = (total * inv_n).astype(BF16)

        with scope(f"ag{it}"):
            near, others = len(rings) - 1, list(range(len(rings) - 1))
            for r in others[:1] + [near] + others[1:]:
                for i in rings[r]:
                    ag_send(it, i)
            raw_q = jnp.dot(p_all[it, me], comp[own], preferred_element_type=F32)
            ag_wait(it, near)
            for i in rings[near]:
                raw_q = raw_q + jnp.dot(p_all[it, peers[i]], comp[i], preferred_element_type=F32)
            for r in others:
                ag_wait(it, r)
        with scope(f"cholesky{it}"):
            gram = jnp.zeros((rank, rank), F32)
            for j in range(n):
                part = p_all[it, j]
                gram = gram + lax.dot_general(part, part, (((1,), (1,)), ((), ())), preferred_element_type=F32)
            terms = terms_in_lanes(inverse_cholesky(gram))
            for r in others:
                for i in rings[r]:
                    raw_q = raw_q + jnp.dot(p_all[it, peers[i]], comp[i], preferred_element_type=F32)

        half = comp.shape[2] // 2

        def q_start_half(stage, h, part):
            along_x = (h + stage) % 2 == 0
            mine_at = my_x if along_x else my_z
            slot = q_x.at[it, stage, h, mine_at]
            slot[...] = part.astype(BF16)
            for d in (2, 1, 3):
                at = lax.rem(mine_at + d, side)
                peer = my_z * side + at if along_x else at * side + my_x
                remote(slot, slot, send_sem.at[3], q_recv_sem.at[it, stage, h], peer).start()

        def q_sum_half(stage, h):
            with scope(f"q_wait{it}_{stage}"):
                held = q_x.at[it, stage, h, pl.ds(0, side - 1)]
                remote(held, held, send_sem.at[3], q_recv_sem.at[it, stage, h], peers[0]).wait_recv()
            return sum(q_x[it, stage, h, s].astype(F32) for s in range(side))

        with scope(f"q_send{it}"):
            left = jnp.concatenate(terms, axis=1)
            hi, mid, low = split3(raw_q)
            zero = jnp.zeros_like(hi)
            right = jnp.concatenate([zero, hi, hi, hi, zero, mid, mid, low], axis=0)
            for h in range(2):
                part = jnp.dot(left, right[:, h * half : (h + 1) * half], preferred_element_type=F32)
                q_start_half(0, h, part)
        if it == ITERS - 1:
            with scope("p_hat"):
                for i in range(n):
                    block = p_all[it, every[i]]
                    block = jnp.concatenate([jnp.zeros_like(block), block, block, block], axis=0)
                    p_hat = jnp.dot(terms[0], block, preferred_element_type=F32).T.astype(BF16)
                    p_out[i] = jnp.concatenate([p_hat, p_hat, p_hat], axis=1)
            small[1].wait()
            b_buf[...] = b0_buf[...].astype(BF16)
            for i, peer in enumerate(peers):
                remote(b_buf.at[peer], b_recv.at[back[i]], send_sem.at[2], b_recv_sem, peer).start()
        for h in range(2):
            q_start_half(1, h, q_sum_half(0, h))
        parts = [q_sum_half(1, h) for h in range(2)]
        factor_q = jnp.concatenate(parts, axis=1) * inv_n
        if it + 1 < ITERS:
            factor_q = factor_q / jnp.sqrt(jnp.sum(factor_q * factor_q, axis=1, keepdims=True) + 1e-06)
            q_half = factor_q.astype(BF16)
        else:
            q_out[...] = factor_q

    with scope("bucket"):
        remote(b_recv, b_recv, send_sem.at[2], b_recv_sem, peers[0]).wait_recv()
        share = b_buf[me].astype(F32)
        for i in range(own):
            share = share + b_recv[i].astype(F32)
        mean_out[...] = share * inv_n
    with scope("sends"):
        blocks = p_all.at[:, pl.ds(0, own)]
        shares = b_buf.at[pl.ds(0, own)]
        halves = q_x.at[:, :, :, pl.ds(0, side - 1)]
        for k, (held, arrived) in enumerate(
            (
                (p_send, rs_recv_sem.at[0, 0]),
                (blocks, ag_recv_sem.at[0, 0]),
                (shares, b_recv_sem),
                (halves, q_recv_sem.at[0, 0, 0]),
            )
        ):
            remote(held, held, send_sem.at[k], arrived, peers[0]).wait_send()


def output_kernel(
    side, comp, p_hat, factor_q, mean, update, new_error, mean_out, u_buf, n_buf, sem, mean_sem
):
    me, _, _, peers = group_of(side)
    every = peers + [me]
    n, rows, _ = comp.shape
    mean_copy = pltpu.make_async_copy(mean, mean_out, mean_sem)
    mean_copy.start()
    right = jnp.concatenate(split3(factor_q[...]), axis=0)
    slots = u_buf.shape[0]
    small = rows // 2
    steps = [[(0, 0, small)], [(0, small, small)], [(1, 0, rows)]]
    steps += [[(i, 0, rows), (i + 1, 0, rows)] for i in range(2, n, 2)]

    def stored(k):
        slot, size = k % slots, pl.ds(0, sum(piece[2] for piece in steps[k]))
        for which, held in enumerate((u_buf.at[slot, size], n_buf.at[slot, size])):
            pltpu.make_async_copy(held, held, sem.at[which, slot]).wait()

    for k, step in enumerate(steps):
        slot = k % slots
        if k >= slots:
            with scope("stores"):
                stored(k - slots)
        with scope("block"):
            at = 0
            for i, r, size in step:
                value = jnp.dot(p_hat[i, r : r + size], right, preferred_element_type=F32)
                u_buf[slot, at : at + size] = value
                n_buf[slot, at : at + size] = (comp[i, r : r + size].astype(F32) - value).astype(BF16)
                at += size
        at = 0
        for i, r, size in step:
            part = pl.ds(pl.multiple_of(every[i] * rows + r, size), size)
            held = pl.ds(at, size)
            pltpu.make_async_copy(u_buf.at[slot, held], update.at[part], sem.at[0, slot]).start()
            pltpu.make_async_copy(n_buf.at[slot, held], new_error.at[part], sem.at[1, slot]).start()
            at += size
    with scope("last"):
        for k in range(max(0, len(steps) - slots), len(steps)):
            stored(k)
    mean_copy.wait()


def in_hbm(array):
    return pltpu.with_memory_space_constraint(array, pltpu.HBM)


def on_device(n, side, grads, error, q_start, bucket):
    depth, width = grads.shape[1:]
    rank = q_start.shape[1]
    rows = depth // n
    shares = bucket.shape[1] // n // 128
    vmem = pl.BlockSpec(memory_space=pltpu.VMEM)
    anywhere = pl.BlockSpec(memory_space=pltpu.HBM)
    sds = jax.ShapeDtypeStruct
    dma = pltpu.SemaphoreType.DMA
    comp, p_hat, factor_q, mean = pl.pallas_call(
        functools.partial(iterate_kernel, n, side),
        out_shape=(
            sds((n, rows, width), BF16),
            sds((n, rows, 3 * rank), BF16),
            sds((rank, width), F32),
            sds((shares, 128), F32),
        ),
        in_specs=[anywhere] * 4,
        out_specs=(vmem, vmem, vmem, vmem),
        scratch_shapes=[
            pltpu.VMEM((n, width, rows), BF16),
            pltpu.VMEM((n, 2, rows, width), BF16),
            pltpu.VMEM((ITERS, n - 1, rank, rows), BF16),
            pltpu.VMEM((ITERS, n - 1, rank, rows), BF16),
            pltpu.VMEM((ITERS, n, rank, rows), BF16),
            pltpu.VMEM((ITERS, 2, 2, side, rank, width // 2), BF16),
            pltpu.VMEM((rank, width), F32),
            pltpu.VMEM((n, shares, 128), F32),
            pltpu.VMEM((n, shares, 128), BF16),
            pltpu.VMEM((n - 1, shares, 128), BF16),
            dma((len(FIRST_RUNS),)),
            dma((2,)),
            dma((4,)),
            dma,
            dma((ITERS, 4)),
            dma((ITERS, 4)),
            dma((ITERS, 2, 2)),
        ],
        compiler_params=pltpu.CompilerParams(
            collective_id=0, has_side_effects=True, vmem_limit_bytes=40 << 20
        ),
        name="iterate",
    )(*(in_hbm(a) for a in (grads[0], error[0], q_start.T, bucket.reshape(n, shares, 128))))

    update, new_error, mean = pl.pallas_call(
        functools.partial(output_kernel, side),
        out_shape=(sds((depth, width), F32), sds((depth, width), BF16), sds((shares, 128), F32)),
        in_specs=[vmem, vmem, vmem, vmem],
        out_specs=(anywhere, anywhere, anywhere),
        scratch_shapes=[
            pltpu.VMEM((4, 2 * rows, width), F32),
            pltpu.VMEM((4, 2 * rows, width), BF16),
            dma((2, 4)),
            dma,
        ],
        compiler_params=pltpu.CompilerParams(vmem_limit_bytes=16 << 20),
        name="outputs",
    )(comp, p_hat, factor_q, mean)
    return update, new_error[None], mean.reshape(-1)


def solution(mesh):
    n = mesh.shape["dp"]
    side = next(s for s in range(1, n + 1) if s * s == n)
    return jax.shard_map(
        functools.partial(on_device, n, side),
        mesh=mesh,
        in_specs=(
            P("dp", None, "expert"),
            P("dp", None, "expert"),
            P("expert", None),
            P("dp", "expert"),
        ),
        out_specs=(P(None, "expert"), P("dp", None, "expert"), P(("expert", "dp"))),
        check_vma=False,
    )
```

```python
import contextlib
import functools

import jax
import jax.numpy as jnp
from jax import lax
from jax.experimental import pallas as pl
from jax.experimental.pallas import tpu as pltpu
from jax.sharding import PartitionSpec as P

ITERS = 2
MESH = pl.DeviceIdType.MESH
F32 = jnp.float32
BF16 = jnp.bfloat16
AHEAD = 6
FIRST_RUNS = (2, 2, 2, 2, 2, 2, 2, 2)
LATER_RUNS = (3, 4, 4, 5)
BARRIER_RUN = 1
TRACE = False


def scope(name):
    return jax.named_scope(name) if TRACE else contextlib.nullcontext()


def runs(items, sizes):
    out = []
    for size in sizes:
        out.append(items[:size])
        items = items[size:]
    assert not items
    return out


def offsets(side):
    near = lambda d: min(d, side - d)
    every = [(dz, dx) for dz in range(side) for dx in range(side) if (dz, dx) != (0, 0)]
    return sorted(every, key=lambda o: (-(near(o[0]) + near(o[1])), o))


def split3(x):
    hi = x.astype(BF16)
    rest = x - hi.astype(F32)
    mid = rest.astype(BF16)
    low = (rest - mid.astype(F32)).astype(BF16)
    return hi, mid, low


def inverse_cholesky(gram, block=8):
    n, lanes, tile = gram.shape[0], 128, 8
    row_id = lax.broadcasted_iota(jnp.int32, (n, lanes), 0)
    lane_id = lax.broadcasted_iota(jnp.int32, (n, lanes), 1)
    eye = ((lane_id >= n) & (lane_id % n == row_id)).astype(F32)
    work = jnp.concatenate([gram, jnp.zeros((n, lanes - n), F32)], axis=1) + eye
    work = [work[tile * i : tile * (i + 1)] for i in range(n // tile)]
    out = [jnp.zeros((tile, lanes), F32) for _ in work]
    tile_row = row_id[:tile]
    for s in range(0, n, block):
        rows = [work[k // tile][k % tile : k % tile + 1] for k in range(s, s + block)]
        pivots = [
            [jnp.broadcast_to(rows[i][:, s + j : s + j + 1], (1, lanes)) for j in range(i + 1)] for i in range(block)
        ]
        rest = range((s + block) // tile, n // tile)
        columns = {
            (t, i): jnp.broadcast_to(work[t][:, s + i : s + i + 1], (tile, lanes)) for t in rest for i in range(block)
        }
        factor, inverse = {}, []
        for p in range(block):
            inverse.append(1.0 / pivots[p][p])
            for i in range(p + 1, block):
                factor[i, p] = pivots[i][p] * inverse[p]
                for j in range(p + 1, i + 1):
                    pivots[i][j] = pivots[i][j] - factor[i, p] * pivots[j][p]
                rows[i] = rows[i] - factor[i, p] * rows[p]
        for p in range(block):
            t, at = divmod(s + p, tile)
            out[t] = jnp.where(tile_row == at, rows[p] / jnp.sqrt(pivots[p][p]), out[t])
        solved = [rows[p] * inverse[p] for p in range(block)]
        for p in reversed(range(block)):
            for i in range(p + 1, block):
                solved[p] = solved[p] - factor[i, p] * solved[i]
        for t in rest:
            for i in range(block):
                work[t] = work[t] - columns[t, i] * solved[i]
    return jnp.concatenate(out, axis=0)


def terms_in_lanes(inverse):
    n = inverse.shape[0]
    part = lax.broadcasted_iota(jnp.int32, inverse.shape, 1) // n
    hi, mid, low = (x.astype(F32) for x in split3(jnp.where(part == 0, 0.0, inverse)))
    start = jnp.where(part == 1, hi, jnp.where(part == 2, mid, 0.0))
    return jnp.where(part == 3, low, start).astype(BF16), jnp.where(part == 3, hi, start).astype(BF16)


def group_of(side):
    me = lax.axis_index("dp")
    my_z, my_x = lax.div(me, side), lax.rem(me, side)
    peers = [lax.rem(my_z + dz, side) * side + lax.rem(my_x + dx, side) for dz, dx in offsets(side)]
    return me, my_z, my_x, peers


def iterate_kernel(
    n,
    side,
    grads,
    error,
    q_start,
    bucket,
    comp,
    p_out,
    q_out,
    mean_out,
    comp_t,
    ge_buf,
    p_send,
    p_recv,
    p_all,
    q_x,
    q0_buf,
    b0_buf,
    b_buf,
    b_recv,
    load_sem,
    small_sem,
    send_sem,
    b_recv_sem,
    rs_recv_sem,
    ag_recv_sem,
    q_recv_sem,
):
    me, my_z, my_x, peers = group_of(side)
    every = peers + [me]
    own = n - 1
    order = offsets(side)
    back = [order.index(((side - dz) % side, (side - dx) % side)) for dz, dx in order]
    steps = [min(dz, side - dz) + min(dx, side - dx) for dz, dx in order]
    rings = [[i for i in range(own) if steps[i] == step] for step in sorted(set(steps), reverse=True)]
    ring_of = [next(r for r, ring in enumerate(rings) if i in ring) for i in range(own)]
    rows = comp.shape[1]
    rank = q_start.shape[0]
    inv_n = 1.0 / n

    def remote(src, dst, send, recv, peer):
        return pltpu.make_async_remote_copy(
            src_ref=src, dst_ref=dst, send_sem=send, recv_sem=recv, device_id={"dp": peer}, device_id_type=MESH
        )

    barrier = pltpu.get_barrier_semaphore()
    for peer in peers:
        pl.semaphore_signal(barrier, inc=1, device_id={"dp": peer}, device_id_type=MESH)

    first_runs = runs(list(range(n)), FIRST_RUNS)
    in_flight = load_sem.shape[0]
    run_of = [next(r for r, run in enumerate(first_runs) if i in run) for i in range(n)]

    def load(i):
        part = pl.ds(pl.multiple_of(every[i] * rows, rows), rows)
        for k, source in enumerate((grads, error)):
            pltpu.make_async_copy(source.at[part], ge_buf.at[i, k], load_sem.at[run_of[i] % in_flight]).start()

    def loaded(r):
        held = ge_buf.at[pl.ds(first_runs[r][0], len(first_runs[r]))]
        pltpu.make_async_copy(held, held, load_sem.at[r % in_flight]).wait()

    small = (
        pltpu.make_async_copy(q_start, q0_buf, small_sem.at[0]),
        pltpu.make_async_copy(bucket, b0_buf, small_sem.at[1]),
    )
    for i in range(AHEAD):
        load(i)
        if i == 0:
            small[0].start()

    def rs_send(it, i):
        remote(
            p_send.at[it, i], p_recv.at[it, back[i]], send_sem.at[0], rs_recv_sem.at[it], peers[i]
        ).start()

    def ag_send(it, i):
        held = p_all.at[it, me]
        remote(held, held, send_sem.at[1], ag_recv_sem.at[it, int(ring_of[i] == len(rings) - 1)], peers[i]).start()

    def ag_wait(it, near):
        count = len(rings[-1]) if near else own - len(rings[-1])
        held = p_all.at[it, pl.ds(0, count)]
        remote(held, held, send_sem.at[1], ag_recv_sem.at[it, near], peers[0]).wait_recv()

    for it in range(ITERS):
        def multiply(run):
            blocks = [jnp.dot(q_half, comp_t[i], preferred_element_type=F32) for i in run]
            for i, part in zip(run, blocks):
                if i != own:
                    p_send[it, i] = part.astype(BF16)
            return blocks[-1]

        def send(run):
            for i in run:
                if i != own:
                    rs_send(it, i)

        with scope(f"p_local{it}"):
            if it == 0:
                before, ready = [], []
                for r, run in enumerate(first_runs):
                    with scope("load"):
                        loaded(r)
                        for i in range(AHEAD + run[0], min(AHEAD + run[-1] + 1, n)):
                            load(i)
                        if r == 1:
                            small[0].wait()
                            q_half = q0_buf[...].astype(BF16)
                    for i in run:
                        comp[i] = ge_buf[i, 0] + ge_buf[i, 1]
                        comp_t[i] = comp[i].T
                    if before:
                        multiply(before)
                        ready = ready + before
                    before = run
                    if r == BARRIER_RUN:
                        with scope("entry"):
                            pl.semaphore_wait(barrier, n - 1)
                    if r >= BARRIER_RUN:
                        send(ready)
                        ready = []
                    if r == len(first_runs) - 2:
                        small[1].start()
                total = multiply(before)
                send(before)
            else:
                for run in runs(list(range(n)), LATER_RUNS):
                    total = multiply(run)
                    send(run)
        with scope(f"rs{it}"):
            remote(p_recv.at[it], p_recv.at[it], send_sem.at[0], rs_recv_sem.at[it], peers[0]).wait_recv()
            for i in range(own):
                total = total + p_recv[it, i].astype(F32)
            p_all[it, me] = (total * inv_n).astype(BF16)

        with scope(f"ag{it}"):
            near, others = len(rings) - 1, list(range(len(rings) - 1))
            for r in others[:1] + [near] + others[1:]:
                for i in rings[r]:
                    ag_send(it, i)
            raw_q = jnp.dot(p_all[it, me], comp[own], preferred_element_type=F32)
            ag_wait(it, 1)
            for i in rings[near]:
                raw_q = raw_q + jnp.dot(p_all[it, peers[i]], comp[i], preferred_element_type=F32)
            ag_wait(it, 0)
        with scope(f"cholesky{it}"):
            gram = jnp.zeros((rank, rank), F32)
            for j in range(n):
                part = p_all[it, j]
                gram = gram + lax.dot_general(part, part, (((1,), (1,)), ((), ())), preferred_element_type=F32)
            terms = terms_in_lanes(inverse_cholesky(gram))
            for r in others:
                for i in rings[r]:
                    raw_q = raw_q + jnp.dot(p_all[it, peers[i]], comp[i], preferred_element_type=F32)

        half = comp.shape[2] // 2

        def q_start_half(stage, h, part):
            along_x = (h + stage) % 2 == 0
            mine_at = my_x if along_x else my_z
            slot = q_x.at[it, stage, h, mine_at]
            slot[...] = part.astype(BF16)
            for d in (2, 1, 3):
                at = lax.rem(mine_at + d, side)
                peer = my_z * side + at if along_x else at * side + my_x
                remote(slot, slot, send_sem.at[3], q_recv_sem.at[it, stage, h], peer).start()

        def q_sum_half(stage, h):
            with scope(f"q_wait{it}_{stage}"):
                held = q_x.at[it, stage, h, pl.ds(0, side - 1)]
                remote(held, held, send_sem.at[3], q_recv_sem.at[it, stage, h], peers[0]).wait_recv()
            return sum(q_x[it, stage, h, s].astype(F32) for s in range(side))

        with scope(f"q_send{it}"):
            left = jnp.concatenate(terms, axis=1)
            hi, mid, low = split3(raw_q)
            zero = jnp.zeros_like(hi)
            right = jnp.concatenate([zero, hi, hi, hi, zero, mid, mid, low], axis=0)
            for h in range(2):
                part = jnp.dot(left, right[:, h * half : (h + 1) * half], preferred_element_type=F32)
                q_start_half(0, h, part)
        if it == ITERS - 1:
            with scope("p_hat"):
                for i in range(n):
                    block = p_all[it, every[i]]
                    block = jnp.concatenate([jnp.zeros_like(block), block, block, block], axis=0)
                    p_hat = jnp.dot(terms[0], block, preferred_element_type=F32).T.astype(BF16)
                    p_out[i] = jnp.concatenate([p_hat, p_hat, p_hat], axis=1)
            small[1].wait()
            b_buf[...] = b0_buf[...].astype(BF16)
            for i, peer in enumerate(peers):
                remote(b_buf.at[peer], b_recv.at[back[i]], send_sem.at[2], b_recv_sem, peer).start()
        for h in range(2):
            q_start_half(1, h, q_sum_half(0, h))
        parts = [q_sum_half(1, h) for h in range(2)]
        factor_q = jnp.concatenate(parts, axis=1) * inv_n
        if it + 1 < ITERS:
            factor_q = factor_q * (1.0 / jnp.sqrt(jnp.sum(factor_q * factor_q, axis=1, keepdims=True) + 1e-06))
            q_half = factor_q.astype(BF16)
        else:
            q_out[...] = factor_q

    with scope("bucket"):
        remote(b_recv, b_recv, send_sem.at[2], b_recv_sem, peers[0]).wait_recv()
        share = b_buf[me].astype(F32)
        for i in range(own):
            share = share + b_recv[i].astype(F32)
        mean_out[...] = share * inv_n
    with scope("sends"):
        blocks = p_all.at[:, pl.ds(0, own)]
        shares = b_buf.at[pl.ds(0, own)]
        halves = q_x.at[:, :, :, pl.ds(0, side - 1)]
        for k, (held, arrived) in enumerate(
            (
                (p_send, rs_recv_sem.at[0]),
                (blocks, ag_recv_sem.at[0, 0]),
                (shares, b_recv_sem),
                (halves, q_recv_sem.at[0, 0, 0]),
            )
        ):
            remote(held, held, send_sem.at[k], arrived, peers[0]).wait_send()


def output_kernel(
    side, comp, p_hat, factor_q, mean, update, new_error, mean_out, u_buf, n_buf, sem, mean_sem
):
    me, _, _, peers = group_of(side)
    every = peers + [me]
    n, rows, _ = comp.shape
    mean_copy = pltpu.make_async_copy(mean, mean_out, mean_sem)
    mean_copy.start()
    right = jnp.concatenate(split3(factor_q[...]), axis=0)
    slots = u_buf.shape[0]
    small = rows // 2
    steps = [[(0, 0, small)], [(0, small, small)], [(1, 0, rows)]]
    steps += [[(i, 0, rows), (i + 1, 0, rows)] for i in range(2, n, 2)]

    def stored(k):
        slot, size = k % slots, pl.ds(0, sum(piece[2] for piece in steps[k]))
        for which, held in enumerate((u_buf.at[slot, size], n_buf.at[slot, size])):
            pltpu.make_async_copy(held, held, sem.at[which, slot]).wait()

    for k, step in enumerate(steps):
        slot = k % slots
        if k >= slots:
            with scope("stores"):
                stored(k - slots)
        with scope("block"):
            at = 0
            for i, r, size in step:
                value = jnp.dot(p_hat[i, r : r + size], right, preferred_element_type=F32)
                u_buf[slot, at : at + size] = value
                n_buf[slot, at : at + size] = (comp[i, r : r + size].astype(F32) - value).astype(BF16)
                at += size
        at = 0
        for i, r, size in step:
            part = pl.ds(pl.multiple_of(every[i] * rows + r, size), size)
            held = pl.ds(at, size)
            pltpu.make_async_copy(u_buf.at[slot, held], update.at[part], sem.at[0, slot]).start()
            pltpu.make_async_copy(n_buf.at[slot, held], new_error.at[part], sem.at[1, slot]).start()
            at += size
    with scope("last"):
        for k in range(max(0, len(steps) - slots), len(steps)):
            stored(k)
    mean_copy.wait()


def in_hbm(array):
    return pltpu.with_memory_space_constraint(array, pltpu.HBM)


def on_device(n, side, grads, error, q_start, bucket):
    depth, width = grads.shape[1:]
    rank = q_start.shape[1]
    rows = depth // n
    shares = bucket.shape[1] // n // 128
    vmem = pl.BlockSpec(memory_space=pltpu.VMEM)
    anywhere = pl.BlockSpec(memory_space=pltpu.HBM)
    sds = jax.ShapeDtypeStruct
    dma = pltpu.SemaphoreType.DMA
    comp, p_hat, factor_q, mean = pl.pallas_call(
        functools.partial(iterate_kernel, n, side),
        out_shape=(
            sds((n, rows, width), BF16),
            sds((n, rows, 3 * rank), BF16),
            sds((rank, width), F32),
            sds((shares, 128), F32),
        ),
        in_specs=[anywhere] * 4,
        out_specs=(vmem, vmem, vmem, vmem),
        scratch_shapes=[
            pltpu.VMEM((n, width, rows), BF16),
            pltpu.VMEM((n, 2, rows, width), BF16),
            pltpu.VMEM((ITERS, n - 1, rank, rows), BF16),
            pltpu.VMEM((ITERS, n - 1, rank, rows), BF16),
            pltpu.VMEM((ITERS, n, rank, rows), BF16),
            pltpu.VMEM((ITERS, 2, 2, side, rank, width // 2), BF16),
            pltpu.VMEM((rank, width), F32),
            pltpu.VMEM((n, shares, 128), F32),
            pltpu.VMEM((n, shares, 128), BF16),
            pltpu.VMEM((n - 1, shares, 128), BF16),
            dma((AHEAD // FIRST_RUNS[0],)),
            dma((2,)),
            dma((4,)),
            dma,
            dma((ITERS,)),
            dma((ITERS, 2)),
            dma((ITERS, 2, 2)),
        ],
        compiler_params=pltpu.CompilerParams(
            collective_id=0, has_side_effects=True, vmem_limit_bytes=40 << 20
        ),
        name="iterate",
    )(*(in_hbm(a) for a in (grads[0], error[0], q_start.T, bucket.reshape(n, shares, 128))))

    update, new_error, mean = pl.pallas_call(
        functools.partial(output_kernel, side),
        out_shape=(sds((depth, width), F32), sds((depth, width), BF16), sds((shares, 128), F32)),
        in_specs=[vmem, vmem, vmem, vmem],
        out_specs=(anywhere, anywhere, anywhere),
        scratch_shapes=[
            pltpu.VMEM((4, 2 * rows, width), F32),
            pltpu.VMEM((4, 2 * rows, width), BF16),
            dma((2, 4)),
            dma,
        ],
        compiler_params=pltpu.CompilerParams(vmem_limit_bytes=16 << 20),
        name="outputs",
    )(comp, p_hat, factor_q, mean)
    return update, new_error[None], mean.reshape(-1)


def solution(mesh):
    n = mesh.shape["dp"]
    side = next(s for s in range(1, n + 1) if s * s == n)
    return jax.shard_map(
        functools.partial(on_device, n, side),
        mesh=mesh,
        in_specs=(
            P("dp", None, "expert"),
            P("dp", None, "expert"),
            P("expert", None),
            P("dp", "expert"),
        ),
        out_specs=(P(None, "expert"), P("dp", None, "expert"), P(("expert", "dp"))),
        check_vma=False,
    )
```

```python
import contextlib
import functools

import jax
import jax.numpy as jnp
from jax import lax
from jax.experimental import pallas as pl
from jax.experimental.pallas import tpu as pltpu
from jax.sharding import PartitionSpec as P

ITERS = 2
MESH = pl.DeviceIdType.MESH
F32 = jnp.float32
BF16 = jnp.bfloat16
AHEAD = 6
FIRST_RUNS = (2, 2, 2, 2, 2, 2, 2, 2)
LATER_RUNS = (3, 4, 4, 5)
BARRIER_RUN = 1
TRACE = False


def scope(name):
    return jax.named_scope(name) if TRACE else contextlib.nullcontext()


def runs(items, sizes):
    out = []
    for size in sizes:
        out.append(items[:size])
        items = items[size:]
    assert not items
    return out


def offsets(side):
    near = lambda d: min(d, side - d)
    every = [(dz, dx) for dz in range(side) for dx in range(side) if (dz, dx) != (0, 0)]
    return sorted(every, key=lambda o: (-(near(o[0]) + near(o[1])), o))


def split3(x):
    hi = x.astype(BF16)
    rest = x - hi.astype(F32)
    mid = rest.astype(BF16)
    low = (rest - mid.astype(F32)).astype(BF16)
    return hi, mid, low


def inverse_cholesky(gram, block=8):
    n, lanes, tile = gram.shape[0], 128, 8
    row_id = lax.broadcasted_iota(jnp.int32, (n, lanes), 0)
    lane_id = lax.broadcasted_iota(jnp.int32, (n, lanes), 1)
    eye = ((lane_id >= n) & (lane_id % n == row_id)).astype(F32)
    work = jnp.concatenate([gram, jnp.zeros((n, lanes - n), F32)], axis=1) + eye
    work = [work[tile * i : tile * (i + 1)] for i in range(n // tile)]
    out = [jnp.zeros((tile, lanes), F32) for _ in work]
    tile_row = row_id[:tile]
    for s in range(0, n, block):
        rows = [work[k // tile][k % tile : k % tile + 1] for k in range(s, s + block)]
        pivots = [
            [jnp.broadcast_to(rows[i][:, s + j : s + j + 1], (1, lanes)) for j in range(i + 1)] for i in range(block)
        ]
        rest = range((s + block) // tile, n // tile)
        columns = {
            (t, i): jnp.broadcast_to(work[t][:, s + i : s + i + 1], (tile, lanes)) for t in rest for i in range(block)
        }
        factor, inverse = {}, []
        for p in range(block):
            inverse.append(1.0 / pivots[p][p])
            for i in range(p + 1, block):
                factor[i, p] = pivots[i][p] * inverse[p]
                for j in range(p + 1, i + 1):
                    pivots[i][j] = pivots[i][j] - factor[i, p] * pivots[j][p]
                rows[i] = rows[i] - factor[i, p] * rows[p]
        for p in range(block):
            t, at = divmod(s + p, tile)
            out[t] = jnp.where(tile_row == at, rows[p] / jnp.sqrt(pivots[p][p]), out[t])
        solved = [rows[p] * inverse[p] for p in range(block)]
        for p in reversed(range(block)):
            for i in range(p + 1, block):
                solved[p] = solved[p] - factor[i, p] * solved[i]
        for t in rest:
            for i in range(block):
                work[t] = work[t] - columns[t, i] * solved[i]
    return jnp.concatenate(out, axis=0)


def terms_in_lanes(inverse):
    n = inverse.shape[0]
    part = lax.broadcasted_iota(jnp.int32, inverse.shape, 1) // n
    hi, mid, low = (x.astype(F32) for x in split3(jnp.where(part == 0, 0.0, inverse)))
    start = jnp.where(part == 1, hi, jnp.where(part == 2, mid, 0.0))
    return jnp.where(part == 3, low, start).astype(BF16), jnp.where(part == 3, hi, start).astype(BF16)


def group_of(side):
    me = lax.axis_index("dp")
    my_z, my_x = lax.div(me, side), lax.rem(me, side)
    peers = [lax.rem(my_z + dz, side) * side + lax.rem(my_x + dx, side) for dz, dx in offsets(side)]
    return me, my_z, my_x, peers


def iterate_kernel(
    n,
    side,
    grads,
    error,
    q_start,
    bucket,
    comp,
    p_out,
    q_out,
    mean_out,
    comp_t,
    ge_buf,
    p_send,
    p_recv,
    p_all,
    q_x,
    q0_buf,
    b0_buf,
    b_buf,
    b_recv,
    load_sem,
    small_sem,
    send_sem,
    b_recv_sem,
    rs_recv_sem,
    ag_recv_sem,
    q_recv_sem,
):
    me, my_z, my_x, peers = group_of(side)
    every = peers + [me]
    own = n - 1
    order = offsets(side)
    back = [order.index(((side - dz) % side, (side - dx) % side)) for dz, dx in order]
    steps = [min(dz, side - dz) + min(dx, side - dx) for dz, dx in order]
    rings = [[i for i in range(own) if steps[i] == step] for step in sorted(set(steps), reverse=True)]
    ring_of = [next(r for r, ring in enumerate(rings) if i in ring) for i in range(own)]
    rows = comp.shape[1]
    rank = q_start.shape[0]
    inv_n = 1.0 / n

    def remote(src, dst, send, recv, peer):
        return pltpu.make_async_remote_copy(
            src_ref=src, dst_ref=dst, send_sem=send, recv_sem=recv, device_id={"dp": peer}, device_id_type=MESH
        )

    barrier = pltpu.get_barrier_semaphore()
    for peer in peers:
        pl.semaphore_signal(barrier, inc=1, device_id={"dp": peer}, device_id_type=MESH)

    first_runs = runs(list(range(n)), FIRST_RUNS)
    run_of = [next(r for r, run in enumerate(first_runs) if i in run) for i in range(n)]

    def load(i):
        part = pl.ds(pl.multiple_of(every[i] * rows, rows), rows)
        for k, source in enumerate((grads, error)):
            pltpu.make_async_copy(source.at[part], ge_buf.at[i, k], load_sem.at[run_of[i]]).start()

    def loaded(r):
        held = ge_buf.at[pl.ds(first_runs[r][0], len(first_runs[r]))]
        pltpu.make_async_copy(held, held, load_sem.at[r]).wait()

    small = (
        pltpu.make_async_copy(q_start, q0_buf, small_sem.at[0]),
        pltpu.make_async_copy(bucket, b0_buf, small_sem.at[1]),
    )
    for i in range(AHEAD):
        load(i)
        if i == 0:
            small[0].start()

    def rs_send(it, i):
        remote(
            p_send.at[it, i], p_recv.at[it, back[i]], send_sem.at[0], rs_recv_sem.at[it, ring_of[i]], peers[i]
        ).start()

    def rs_wait(it, r):
        held = p_recv.at[it, pl.ds(rings[r][0], len(rings[r]))]
        remote(held, held, send_sem.at[0], rs_recv_sem.at[it, r], peers[0]).wait_recv()

    def ag_send(it, i):
        held = p_all.at[it, me]
        remote(held, held, send_sem.at[1], ag_recv_sem.at[it, ring_of[i]], peers[i]).start()

    def ag_wait(it, r):
        held = p_all.at[it, pl.ds(0, len(rings[r]))]
        remote(held, held, send_sem.at[1], ag_recv_sem.at[it, r], peers[0]).wait_recv()

    for it in range(ITERS):
        def multiply(run):
            blocks = [jnp.dot(q_half, comp_t[i], preferred_element_type=F32) for i in run]
            for i, part in zip(run, blocks):
                if i != own:
                    p_send[it, i] = part.astype(BF16)
            return blocks[-1]

        def send(run):
            for i in run:
                if i != own:
                    rs_send(it, i)

        with scope(f"p_local{it}"):
            if it == 0:
                before, ready = [], []
                for r, run in enumerate(first_runs):
                    with scope("load"):
                        loaded(r)
                        for i in range(AHEAD + run[0], min(AHEAD + run[-1] + 1, n)):
                            load(i)
                        if r == 1:
                            small[0].wait()
                            q_half = q0_buf[...].astype(BF16)
                    for i in run:
                        comp[i] = ge_buf[i, 0] + ge_buf[i, 1]
                        comp_t[i] = comp[i].T
                    if before:
                        multiply(before)
                        ready = ready + before
                    before = run
                    if r == BARRIER_RUN:
                        with scope("entry"):
                            pl.semaphore_wait(barrier, n - 1)
                    if r >= BARRIER_RUN:
                        send(ready)
                        ready = []
                    if r == len(first_runs) - 2:
                        small[1].start()
                total = multiply(before)
                send(before)
            else:
                for run in runs(list(range(n)), LATER_RUNS):
                    total = multiply(run)
                    send(run)
        with scope(f"rs{it}"):
            for r in reversed(range(len(rings))):
                rs_wait(it, r)
                for i in rings[r]:
                    total = total + p_recv[it, i].astype(F32)
            p_all[it, me] = (total * inv_n).astype(BF16)

        with scope(f"ag{it}"):
            near, others = len(rings) - 1, list(range(len(rings) - 1))
            for r in others[:1] + [near] + others[1:]:
                for i in rings[r]:
                    ag_send(it, i)
            raw_q = jnp.dot(p_all[it, me], comp[own], preferred_element_type=F32)
            ag_wait(it, near)
            for i in rings[near]:
                raw_q = raw_q + jnp.dot(p_all[it, peers[i]], comp[i], preferred_element_type=F32)
            for r in others:
                ag_wait(it, r)
        with scope(f"cholesky{it}"):
            gram = jnp.zeros((rank, rank), F32)
            for j in range(n):
                part = p_all[it, j]
                gram = gram + lax.dot_general(part, part, (((1,), (1,)), ((), ())), preferred_element_type=F32)
            terms = terms_in_lanes(inverse_cholesky(gram))
            for r in others:
                for i in rings[r]:
                    raw_q = raw_q + jnp.dot(p_all[it, peers[i]], comp[i], preferred_element_type=F32)

        half = comp.shape[2] // 2

        def q_start_half(stage, h, part):
            along_x = (h + stage) % 2 == 0
            mine_at = my_x if along_x else my_z
            slot = q_x.at[it, stage, h, mine_at]
            slot[...] = part.astype(BF16)
            for d in (2, 1, 3):
                at = lax.rem(mine_at + d, side)
                peer = my_z * side + at if along_x else at * side + my_x
                remote(slot, slot, send_sem.at[3], q_recv_sem.at[it, stage, h], peer).start()

        def q_sum_half(stage, h):
            with scope(f"q_wait{it}_{stage}"):
                held = q_x.at[it, stage, h, pl.ds(0, side - 1)]
                remote(held, held, send_sem.at[3], q_recv_sem.at[it, stage, h], peers[0]).wait_recv()
            return sum(q_x[it, stage, h, s].astype(F32) for s in range(side))

        with scope(f"q_send{it}"):
            left = jnp.concatenate(terms, axis=1)
            hi, mid, low = split3(raw_q)
            zero = jnp.zeros_like(hi)
            right = jnp.concatenate([zero, hi, hi, hi, zero, mid, mid, low], axis=0)
            for h in range(2):
                part = jnp.dot(left, right[:, h * half : (h + 1) * half], preferred_element_type=F32)
                q_start_half(0, h, part)
        if it == ITERS - 1:
            with scope("p_hat"):
                for i in range(n):
                    block = p_all[it, every[i]]
                    block = jnp.concatenate([jnp.zeros_like(block), block, block, block], axis=0)
                    p_hat = jnp.dot(terms[0], block, preferred_element_type=F32).T.astype(BF16)
                    p_out[i] = jnp.concatenate([p_hat, p_hat, p_hat], axis=1)
            small[1].wait()
            b_buf[...] = b0_buf[...].astype(BF16)
            for i, peer in enumerate(peers):
                remote(b_buf.at[peer], b_recv.at[back[i]], send_sem.at[2], b_recv_sem, peer).start()
        for h in range(2):
            q_start_half(1, h, q_sum_half(0, h))
        parts = [q_sum_half(1, h) for h in range(2)]
        factor_q = jnp.concatenate(parts, axis=1) * inv_n
        if it + 1 < ITERS:
            factor_q = factor_q / jnp.sqrt(jnp.sum(factor_q * factor_q, axis=1, keepdims=True) + 1e-06)
            q_half = factor_q.astype(BF16)
        else:
            q_out[...] = factor_q

    with scope("bucket"):
        remote(b_recv, b_recv, send_sem.at[2], b_recv_sem, peers[0]).wait_recv()
        share = b_buf[me].astype(F32)
        for i in range(own):
            share = share + b_recv[i].astype(F32)
        mean_out[...] = share * inv_n
    with scope("sends"):
        blocks = p_all.at[:, pl.ds(0, own)]
        shares = b_buf.at[pl.ds(0, own)]
        halves = q_x.at[:, :, :, pl.ds(0, side - 1)]
        for k, (held, arrived) in enumerate(
            (
                (p_send, rs_recv_sem.at[0, 0]),
                (blocks, ag_recv_sem.at[0, 0]),
                (shares, b_recv_sem),
                (halves, q_recv_sem.at[0, 0, 0]),
            )
        ):
            remote(held, held, send_sem.at[k], arrived, peers[0]).wait_send()


def output_kernel(
    side, comp, p_hat, factor_q, mean, update, new_error, mean_out, u_buf, n_buf, sem, mean_sem
):
    me, _, _, peers = group_of(side)
    every = peers + [me]
    n, rows, _ = comp.shape
    mean_copy = pltpu.make_async_copy(mean, mean_out, mean_sem)
    mean_copy.start()
    right = jnp.concatenate(split3(factor_q[...]), axis=0)
    slots = u_buf.shape[0]
    small = rows // 2
    steps = [[(0, 0, small)], [(0, small, small)], [(1, 0, rows)]]
    steps += [[(i, 0, rows), (i + 1, 0, rows)] for i in range(2, n, 2)]

    def stored(k):
        slot, size = k % slots, pl.ds(0, sum(piece[2] for piece in steps[k]))
        for which, held in enumerate((u_buf.at[slot, size], n_buf.at[slot, size])):
            pltpu.make_async_copy(held, held, sem.at[which, slot]).wait()

    for k, step in enumerate(steps):
        slot = k % slots
        if k >= slots:
            with scope("stores"):
                stored(k - slots)
        with scope("block"):
            at = 0
            for i, r, size in step:
                value = jnp.dot(p_hat[i, r : r + size], right, preferred_element_type=F32)
                u_buf[slot, at : at + size] = value
                n_buf[slot, at : at + size] = (comp[i, r : r + size].astype(F32) - value).astype(BF16)
                at += size
        at = 0
        for i, r, size in step:
            part = pl.ds(pl.multiple_of(every[i] * rows + r, size), size)
            held = pl.ds(at, size)
            pltpu.make_async_copy(u_buf.at[slot, held], update.at[part], sem.at[0, slot]).start()
            pltpu.make_async_copy(n_buf.at[slot, held], new_error.at[part], sem.at[1, slot]).start()
            at += size
    with scope("last"):
        for k in range(max(0, len(steps) - slots), len(steps)):
            stored(k)
    mean_copy.wait()


def in_hbm(array):
    return pltpu.with_memory_space_constraint(array, pltpu.HBM)


def on_device(n, side, grads, error, q_start, bucket):
    depth, width = grads.shape[1:]
    rank = q_start.shape[1]
    rows = depth // n
    shares = bucket.shape[1] // n // 128
    vmem = pl.BlockSpec(memory_space=pltpu.VMEM)
    anywhere = pl.BlockSpec(memory_space=pltpu.HBM)
    sds = jax.ShapeDtypeStruct
    dma = pltpu.SemaphoreType.DMA
    comp, p_hat, factor_q, mean = pl.pallas_call(
        functools.partial(iterate_kernel, n, side),
        out_shape=(
            sds((n, rows, width), BF16),
            sds((n, rows, 3 * rank), BF16),
            sds((rank, width), F32),
            sds((shares, 128), F32),
        ),
        in_specs=[anywhere] * 4,
        out_specs=(vmem, vmem, vmem, vmem),
        scratch_shapes=[
            pltpu.VMEM((n, width, rows), BF16),
            pltpu.VMEM((n, 2, rows, width), BF16),
            pltpu.VMEM((ITERS, n - 1, rank, rows), BF16),
            pltpu.VMEM((ITERS, n - 1, rank, rows), BF16),
            pltpu.VMEM((ITERS, n, rank, rows), BF16),
            pltpu.VMEM((ITERS, 2, 2, side, rank, width // 2), BF16),
            pltpu.VMEM((rank, width), F32),
            pltpu.VMEM((n, shares, 128), F32),
            pltpu.VMEM((n, shares, 128), BF16),
            pltpu.VMEM((n - 1, shares, 128), BF16),
            dma((len(FIRST_RUNS),)),
            dma((2,)),
            dma((4,)),
            dma,
            dma((ITERS, 4)),
            dma((ITERS, 4)),
            dma((ITERS, 2, 2)),
        ],
        compiler_params=pltpu.CompilerParams(
            collective_id=0, has_side_effects=True, vmem_limit_bytes=40 << 20
        ),
        name="iterate",
    )(*(in_hbm(a) for a in (grads[0], error[0], q_start.T, bucket.reshape(n, shares, 128))))

    update, new_error, mean = pl.pallas_call(
        functools.partial(output_kernel, side),
        out_shape=(sds((depth, width), F32), sds((depth, width), BF16), sds((shares, 128), F32)),
        in_specs=[vmem, vmem, vmem, vmem],
        out_specs=(anywhere, anywhere, anywhere),
        scratch_shapes=[
            pltpu.VMEM((4, 2 * rows, width), F32),
            pltpu.VMEM((4, 2 * rows, width), BF16),
            dma((2, 4)),
            dma,
        ],
        compiler_params=pltpu.CompilerParams(vmem_limit_bytes=16 << 20),
        name="outputs",
    )(comp, p_hat, factor_q, mean)
    return update, new_error[None], mean.reshape(-1)


def solution(mesh):
    n = mesh.shape["dp"]
    side = next(s for s in range(1, n + 1) if s * s == n)
    return jax.shard_map(
        functools.partial(on_device, n, side),
        mesh=mesh,
        in_specs=(
            P("dp", None, "expert"),
            P("dp", None, "expert"),
            P("expert", None),
            P("dp", "expert"),
        ),
        out_specs=(P(None, "expert"), P("dp", None, "expert"), P(("expert", "dp"))),
        check_vma=False,
    )
```
